128 devices in a mesh: seq: 32 (over z, x_lo, y), head: 4 (over x_hi, core).
Axes of the slice: x: 4 (x_hi: 2, x_lo: 2; x = x_hi * 2 + x_lo), y: 4, z: 4, core: 2. Of those that a mesh axis runs over, the one named last changes fastest.
Arguments:
- hidden_in: bfloat16 [12, 2048, 1024], P(None, 'seq'), may hold values from -48 to 48
- lengths: int32 [12], replicated, may hold values from 1 to 2048, as said below
- w_qkv: float32 [1024, 3072], P(('seq', 'head')), may hold values from -0.1875 to 0.1875
- w_attn_out: float32 [1024, 1024], P(('seq', 'head')), may hold values from -0.1875 to 0.1875
- w_in: float32 [1024, 4096], P(('seq', 'head')), may hold values from -0.1875 to 0.1875
- w_down: float32 [4096, 1024], P(('seq', 'head')), may hold values from -0.09375 to 0.09375
- ln_gain: float32 [2, 1024], replicated, may hold values from 0.5 to 1.5
- ln_bias: float32 [2, 1024], replicated, may hold values from -1.5 to 1.5
Outputs:
- hidden_out: bfloat16 [12, 2048, 1024], P(None, 'seq', 'head')
- key_cache: bfloat16 [12, 2048, 1024], P(None, 'seq', 'head')
- value_cache: bfloat16 [12, 2048, 1024], P(None, 'seq', 'head')
The draws below stay inside these ranges and needn't reach their ends.
Inputs may be any that keep to these rules, and one draw needn't show every extreme that they name: `lengths`: the longest prompt has exactly 2048 positions.
All inputs are finite; a program needn't handle non-finite values.
Results may differ from the reference program's by a relative error of at most 0.014.
Values may be sent and summed in bfloat16 or wider, within the bound.
A program may use at most 192 MiB of HBM per device.

```python
import jax
import jax.numpy as jnp
from jax import lax

D = 1024
HEADS = 16
HEAD_DIM = 64
FF = 4096
PROMPTS = 12
SLEN = 2048


def prompt_lengths(key):
    key_values = jax.random.fold_in(key, 21)
    key_pick = jax.random.fold_in(key, 22)
    drawn = jax.random.randint(key_values, (PROMPTS,), 1, SLEN + 1)
    chosen = jax.random.randint(key_pick, (), 0, PROMPTS)
    return jnp.where(jnp.arange(PROMPTS) == chosen, SLEN, drawn).astype(jnp.int32)


def draw_hidden_in(key, part):
    key_base = jax.random.fold_in(key, 11)
    base = jax.random.truncated_normal(key_base, -4.0, 4.0, (PROMPTS, SLEN, D), jnp.float32)
    return base.astype(jnp.bfloat16)


def draw_lengths(key, part):
    return prompt_lengths(key)


def block_levels(own_key, extent, shards, low, largest):
    level, own = 1.0, jax.random.fold_in(own_key, 6)
    for dim, blocks in shards:
        draws = jnp.exp(jax.random.uniform(jax.random.fold_in(own, dim), (blocks,), jnp.float32, low / len(shards), largest / len(shards)))
        level = level * jnp.repeat(draws, extent[dim] // blocks).reshape([-1 if axis == dim else 1 for axis in range(len(extent))])
    return level


def normal_values(stream_key, extent, width, limit, cuts=(), kind=jnp.bfloat16):
    factor_of = block_levels(stream_key, extent, cuts, -0.22, 0.18) if cuts else 1.0
    entries = jax.random.normal(stream_key, extent, jnp.float32) * width * factor_of
    return jnp.minimum(jnp.maximum(entries, -limit), limit).astype(kind)


def setup_inputs(seed: int = 0) -> dict:
    seeds = jax.random.split(jax.random.key(seed), 9)
    hidden_in = draw_hidden_in(jax.random.fold_in(seeds[8], 71), 0)
    lengths = draw_lengths(jax.random.fold_in(seeds[8], 71), 0)
    w_qkv = normal_values(seeds[2], (D, 3 * D), D ** -0.5, 0.1875, ((0, 128),), jnp.float32)
    w_attn_out = normal_values(seeds[3], (D, D), D ** -0.5, 0.1875, ((0, 128),), jnp.float32)
    w_in = normal_values(seeds[4], (D, FF), D ** -0.5, 0.1875, ((0, 128),), jnp.float32)
    w_down = normal_values(seeds[5], (FF, D), FF ** -0.5, 0.09375, ((0, 128),), jnp.float32)
    ln_gain = jnp.clip(1.0 + 0.1 * jax.random.normal(seeds[6], (2, D), jnp.float32), 0.5, 1.5)
    ln_bias = normal_values(seeds[7], (2, D), 0.3, 1.5, (), jnp.float32)
    return dict(hidden_in=hidden_in, lengths=lengths, w_qkv=w_qkv, w_attn_out=w_attn_out, w_in=w_in, w_down=w_down, ln_gain=ln_gain, ln_bias=ln_bias)


EPSILON = 1e-05

def normalize(row_values, gain_row, shift_row):
    average = lax.optimization_barrier(jnp.mean(row_values, axis=-1, keepdims=True))
    squares = lax.optimization_barrier(jnp.mean(row_values * row_values, axis=-1, keepdims=True))
    spread = squares - average * average
    return (row_values - average) * lax.rsqrt(spread + EPSILON) * gain_row + shift_row

def reference(hidden_in, lengths, w_qkv, w_attn_out, w_in, w_down, ln_gain, ln_bias):
    qkv_weight = w_qkv.astype(jnp.bfloat16)
    out_weight = w_attn_out.astype(jnp.bfloat16)
    in_weight = w_in.astype(jnp.bfloat16)
    down_weight = w_down.astype(jnp.bfloat16)
    token_rows = hidden_in.reshape(PROMPTS * SLEN, D)
    projected = jnp.dot(token_rows, qkv_weight, preferred_element_type=jnp.float32).astype(jnp.bfloat16)
    projected = projected.reshape(PROMPTS, SLEN, 3, HEADS, HEAD_DIM)
    positions = jnp.arange(SLEN, dtype=jnp.int32)
    live_mask = positions[None, :] < lengths[:, None].astype(jnp.int32)
    queries = projected[:, :, 0]
    zero_value = jnp.zeros((), jnp.bfloat16)
    key_cache = jnp.where(live_mask[:, :, None, None], projected[:, :, 1], zero_value)
    value_cache = jnp.where(live_mask[:, :, None, None], projected[:, :, 2], zero_value)
    score_scale = HEAD_DIM ** (-0.5)

    def one_prompt(prompt_items):
        query_rows, key_rows, value_rows, key_live = prompt_items
        scores = jnp.einsum('qhd,khd->hqk', query_rows.astype(jnp.float32), key_rows.astype(jnp.float32)) * score_scale
        scores = jnp.where(key_live[None, None, :], scores, -jnp.inf)
        row_max = lax.optimization_barrier(jnp.max(scores, axis=-1, keepdims=True))
        exp_terms = jnp.exp(scores - row_max)
        soft_weights = (exp_terms / lax.optimization_barrier(jnp.sum(exp_terms, axis=-1, keepdims=True))).astype(jnp.bfloat16)
        head_mix = jnp.einsum('hqk,khd->qhd', soft_weights.astype(jnp.float32), value_rows.astype(jnp.float32))
        return head_mix.astype(jnp.bfloat16)
    attended = lax.map(one_prompt, (queries, key_cache, value_cache, live_mask))
    attended = attended.reshape(PROMPTS * SLEN, D)
    attn_sum = jnp.dot(attended, out_weight, preferred_element_type=jnp.float32) + token_rows.astype(jnp.float32)
    normed = normalize(attn_sum, ln_gain[0], ln_bias[0]).astype(jnp.bfloat16)
    hidden_units = jax.nn.gelu(jnp.dot(normed, in_weight, preferred_element_type=jnp.float32), approximate=False).astype(jnp.bfloat16)
    ffn_sum = jnp.dot(hidden_units, down_weight, preferred_element_type=jnp.float32) + normed.astype(jnp.float32)
    hidden_out = normalize(ffn_sum, ln_gain[1], ln_bias[1]).astype(jnp.bfloat16)
    return (hidden_out.reshape(PROMPTS, SLEN, D), key_cache.reshape(PROMPTS, SLEN, D), value_cache.reshape(PROMPTS, SLEN, D))
```

```python
import functools
import math

import jax
import jax.numpy as jnp
from jax import lax
from jax.experimental import pallas as pl
from jax.experimental.pallas import tpu as pltpu
from jax.sharding import PartitionSpec as P

MESH = pl.DeviceIdType.MESH
BF = jnp.bfloat16
F32 = jnp.float32
EPSILON = 1e-05
SCORE_FACTOR = 64 ** (-0.5) * math.log2(math.e)
DEAD = -1e30


class Place:
    def __init__(self):
        self.s = lax.axis_index("seq")
        self.h = lax.axis_index("head")
        self.z = self.s // 8
        self.xl = lax.rem(self.s // 4, 2)
        self.y = lax.rem(self.s, 4)
        self.xh = self.h // 2
        self.c = lax.rem(self.h, 2)
        self.x = self.xh * 2 + self.xl

    def peer(self, dim, d):
        x, y, z = self.x, self.y, self.z
        if dim == "x":
            x = lax.rem(x + d, 4)
        elif dim == "y":
            y = lax.rem(y + d, 4)
        else:
            z = lax.rem(z + d, 4)
        return (z * 8 + lax.rem(x, 2) * 4 + y, (x // 2) * 2 + self.c)

    def sibling(self):
        return (self.s, self.xh * 2 + 1 - self.c)


def duty(s):
    z, xl, y = s // 8, lax.rem(s // 4, 2), lax.rem(s, 4)
    r = lax.rem(y + z, 4)
    return z * 3 + r, xl, r < 3


def remote(src, dst, send, recv, device):
    return pltpu.make_async_remote_copy(
        src_ref=src, dst_ref=dst, send_sem=send, recv_sem=recv, device_id=device, device_id_type=MESH
    )


def greet(barrier, device):
    pl.semaphore_signal(barrier, inc=1, device_id=device, device_id_type=MESH)


def project_kernel(
    x_ref, w_ref, len_ref, kc_ref, vc_ref, qkv_ref,
    other, theirs, slab, weight, outbox,
    pair_sem, one_send, one_recv, two_send, two_recv, three_send, three_recv, own_sem, box_send, box_recv,
):
    me = Place()
    barrier = pltpu.get_barrier_semaphore()

    def greet_seq(i, carry):
        greet(barrier, (lax.rem(me.s + i, 32), me.h))
        return carry

    lax.fori_loop(1, 32, greet_seq, 0)
    greet(barrier, me.sibling())
    for xl in range(2):
        greet(barrier, (me.z * 8 + xl * 4 + me.y, (1 - me.xh) * 2 + me.c))

    for k in range(2):
        for t in range(3):
            at = pl.multiple_of(t * 1024 + (2 * k + 1 - me.c) * 256, 256)
            other[:, k * 768 + t * 256 : k * 768 + (t + 1) * 256] = w_ref[:, pl.ds(at, 256)]
    pl.semaphore_wait(barrier, 34)
    swap = remote(other, theirs, pair_sem.at[0], pair_sem.at[1], me.sibling())
    swap.start()
    swap.wait()
    first = me.c == 0
    for k in range(2):
        for t in range(3):
            at = pl.multiple_of(t * 1024 + (2 * k + me.c) * 256, 256)
            mine = w_ref[:, pl.ds(at, 256)]
            sent = theirs[:, k * 768 + t * 256 : k * 768 + (t + 1) * 256]
            rows = jnp.concatenate([jnp.where(first, mine, sent), jnp.where(first, sent, mine)], axis=0)
            slab[k, :, t * 256 : (t + 1) * 256] = rows.astype(BF)
    weight[me.z, me.xl, me.y, me.xh] = slab[me.xh]

    one = []
    for d in range(1, 4):
        target = me.peer("x", d)
        copy = remote(
            slab.at[target[1] // 2],
            weight.at[me.z, me.xl, me.y, me.xh],
            one_send.at[d - 1],
            one_recv.at[d - 1],
            target,
        )
        copy.start()
        one.append(copy)
    for copy in one:
        copy.wait_recv()

    left, right = pl.ds(0, 384), pl.ds(384, 384)
    all2, all4, all16 = pl.ds(0, 2), pl.ds(0, 4), pl.ds(0, 16)
    zs, ys = pl.ds(me.z, 1), pl.ds(me.y, 1)
    two = []
    for d in range(1, 4):
        for k, (dim, cols) in enumerate((("y", left), ("z", right))):
            part = weight.at[zs, all2, ys, all2, all16, cols]
            copy = remote(part, part, two_send.at[k, d - 1], two_recv.at[k, d - 1], me.peer(dim, d))
            copy.start()
            two.append(copy)
    for copy in two:
        copy.wait_recv()
    three = []
    for d in range(1, 4):
        for k, dim in enumerate(("z", "y")):
            if k == 0:
                part = weight.at[zs, all2, all4, all2, all16, left]
            else:
                part = weight.at[all4, all2, ys, all2, all16, right]
            copy = remote(part, part, three_send.at[k, d - 1], three_recv.at[k, d - 1], me.peer(dim, d))
            copy.start()
            three.append(copy)
    for copy in three:
        copy.wait_recv()

    for t in range(3):
        w = weight[:, :, :, :, :, t * 256 : (t + 1) * 256].reshape(1024, 256)
        for g in range(2):
            rows = x_ref[g * 6 : (g + 1) * 6].reshape(384, 1024)
            got = jnp.dot(rows, w, preferred_element_type=F32)
            for q in range(6):
                p = g * 6 + q
                piece = got[q * 64 : (q + 1) * 64]
                if t > 0:
                    at = me.s * 64 + lax.broadcasted_iota(jnp.int32, (64, 256), 0)
                    piece = jnp.where(at < len_ref[p], piece, 0.0)
                piece = piece.astype(BF)
                if t == 1:
                    kc_ref[p] = piece
                if t == 2:
                    vc_ref[p] = piece
                outbox[p * 2, t] = piece[:, :128]
                outbox[p * 2 + 1, t] = piece[:, 128:]

    prompt, pair, busy = duty(me.s)

    def post(i, carry):
        to = lax.rem(me.s + i, 32)
        their_prompt, their_pair, their_busy = duty(to)

        @pl.when(their_busy)
        def _():
            remote(
                outbox.at[their_prompt * 2 + their_pair], qkv_ref.at[:, me.s], box_send, box_recv, (to, me.h)
            ).start()

        return carry

    lax.fori_loop(1, 32, post, 0)

    @pl.when(busy)
    def _():
        keep = pltpu.make_async_copy(outbox.at[prompt * 2 + pair], qkv_ref.at[:, me.s], own_sem)
        keep.start()
        keep.wait()
        arrived = qkv_ref.at[:, pl.ds(0, 31)]
        pltpu.make_async_copy(arrived, arrived, box_recv).wait()
        gone = outbox.at[pl.ds(0, 23)]
        pltpu.make_async_copy(gone, gone, box_send).wait()

    @pl.when(jnp.logical_not(busy))
    def _():
        gone = outbox.at[pl.ds(0, 24)]
        pltpu.make_async_copy(gone, gone, box_send).wait()

    for copy in one + two + three:
        copy.wait_send()


def project(x, w_qkv, lengths):
    vmem, hbm = pl.BlockSpec(memory_space=pltpu.VMEM), pl.BlockSpec(memory_space=pl.ANY)
    dma = pltpu.SemaphoreType.DMA
    return pl.pallas_call(
        project_kernel,
        out_shape=(
            jax.ShapeDtypeStruct((12, 64, 256), BF),
            jax.ShapeDtypeStruct((12, 64, 256), BF),
            jax.ShapeDtypeStruct((3, 32, 64, 128), BF),
        ),
        in_specs=[vmem, vmem, pl.BlockSpec(memory_space=pltpu.SMEM)],
        out_specs=(vmem, vmem, hbm),
        scratch_shapes=[
            pltpu.VMEM((8, 1536), F32),
            pltpu.VMEM((8, 1536), F32),
            pltpu.VMEM((2, 16, 768), BF),
            pltpu.VMEM((4, 2, 4, 2, 16, 768), BF),
            pltpu.VMEM((24, 3, 64, 128), BF),
            dma((2,)),
            dma((3,)),
            dma((3,)),
            dma((2, 3)),
            dma((2, 3)),
            dma((2, 3)),
            dma((2, 3)),
            dma,
            dma,
            dma,
        ],
        compiler_params=pltpu.CompilerParams(collective_id=0, has_side_effects=True, vmem_limit_bytes=48 << 20),
    )(x, w_qkv, lengths)


def normalize(rows, gain, shift):
    average = jnp.mean(rows, axis=1, keepdims=True)
    spread = jnp.mean(rows * rows, axis=1, keepdims=True) - average * average
    return (rows - average) * lax.rsqrt(spread + EPSILON) * gain + shift


def layer_kernel(
    qkv_ref, x_ref, len_ref, out_f32, in_f32, down_f32, gain_ref, bias_ref, hidden_ref,
    in_half, out_half, w_in, w_out, w_down, q_aug, k_aug, v_aug, attended, joined, hidden, result,
    swap_send, swap_recv, ring_send, ring_recv, share_send, share_recv,
    mix_send, mix_recv, mix_own, last_send, last_recv,
):
    me = Place()
    prompt, pair, busy = duty(me.s)
    barrier = pltpu.get_barrier_semaphore()
    rank = me.s * 4 + me.h

    def greet_all(i, carry):
        to = lax.rem(rank + i, 128)
        greet(barrier, (to // 4, lax.rem(to, 4)))
        return carry

    lax.fori_loop(1, 128, greet_all, 0)
    pl.semaphore_wait(barrier, 127)

    sibling = me.sibling()
    there = 1 - me.c
    swaps = [
        remote(
            out_f32.at[:, pl.ds(pl.multiple_of(there * 512, 512), 512)],
            out_half, swap_send.at[0], swap_recv.at[0], sibling,
        ),
        remote(
            in_f32.at[:, pl.ds(pl.multiple_of(there * 2048, 2048), 2048)],
            in_half, swap_send.at[1], swap_recv.at[1], sibling,
        ),
    ]
    for copy in swaps:
        copy.start()
    w_down[me.z, me.xl, me.y, me.xh, me.c] = down_f32[...].astype(BF)
    for copy in swaps:
        copy.wait_recv()
    first = me.c == 0
    for source, half, width, target in ((out_f32, out_half, 512, w_out), (in_f32, in_half, 2048, w_in)):
        mine = source[:, pl.ds(pl.multiple_of(me.c * width, width), width)]
        sent = half[...]
        rows = jnp.concatenate([jnp.where(first, mine, sent), jnp.where(first, sent, mine)], axis=0)
        target[me.c, me.z, me.xl, me.y, me.xh] = rows.astype(BF)

    one_c = pl.ds(me.c, 1)

    def region(piece, zs, xls, ys, xhs):
        rows16, rows32 = pl.ds(0, 16), pl.ds(0, 32)
        if piece == 0:
            return w_in.at[one_c, zs, xls, ys, xhs, rows16, pl.ds(0, 1536)]
        if piece == 1:
            return w_out.at[one_c, zs, xls, ys, xhs, rows16, pl.ds(0, 512)]
        if piece == 2:
            return w_in.at[one_c, zs, xls, ys, xhs, rows16, pl.ds(1536, 512)]
        if piece == 3:
            return w_down.at[zs, xls, ys, xhs, one_c, rows32, pl.ds(768, 256)]
        return w_down.at[zs, xls, ys, xhs, one_c, rows32, pl.ds(0, 768)]

    order = {0: "xyz", 1: "yzx", 2: "yzx", 3: "yzx", 4: "zxy"}
    pieces = (1, 0, 2, 3, 4)

    def area(piece, done, at=None):
        x, y, z = me.x, me.y, me.z
        if at is not None:
            dim, d = at
            x = lax.rem(x + d, 4) if dim == "x" else x
            y = lax.rem(y + d, 4) if dim == "y" else y
            z = lax.rem(z + d, 4) if dim == "z" else z
        zs = pl.ds(0, 4) if "z" in done else pl.ds(z, 1)
        ys = pl.ds(0, 4) if "y" in done else pl.ds(y, 1)
        xls = pl.ds(0, 2) if "x" in done else pl.ds(lax.rem(x, 2), 1)
        xhs = pl.ds(0, 2) if "x" in done else pl.ds(x // 2, 1)
        return region(piece, zs, xls, ys, xhs)

    pending = []

    def send_phase(phase):
        started = []
        for piece in pieces:
            dims = order[piece]
            part = area(piece, dims[:phase])
            for d in (1, 3, 2):
                copy = remote(
                    part, part, ring_send.at[piece, phase, d - 1], ring_recv.at[piece, phase, d - 1],
                    me.peer(dims[phase], d),
                )
                copy.start()
                started.append((piece, d, copy))
                pending.append(copy)
        return started

    shares = []

    def share(piece, slot, part):
        copy = remote(part, part, share_send.at[piece, slot], share_recv.at[piece, slot], sibling)
        copy.start()
        shares.append(copy)
        pending.append(copy)

    lane = lax.broadcasted_iota(jnp.int32, (2048, 128), 1)

    @pl.when(busy)
    def _():
        place = lax.broadcasted_iota(jnp.int32, (2048, 128), 0)
        bias = jnp.where(place < len_ref[prompt], 0.0, DEAD)
        q = qkv_ref[0].reshape(2048, 128).astype(F32)
        k = qkv_ref[1].reshape(2048, 128).astype(F32)
        v = qkv_ref[2].reshape(2048, 128).astype(F32)
        for n in range(2):
            own = (lane // 64) == n
            mark = lane == (1 - n) * 64
            q_aug[n] = jnp.where(own, q, jnp.where(mark, 1.0, 0.0)).astype(BF)
            k_aug[n] = jnp.where(mark, bias, k).astype(BF)
            v_aug[n] = jnp.where(own, v, 1.0).astype(BF)

    low = lax.broadcasted_iota(jnp.int32, (256, 128), 1) < 64

    def attend(start, stop):
        @pl.when(busy)
        def _():
            def block(i, carry):
                rows = pl.ds(pl.multiple_of(i * 256, 256), 256)
                mixed = []
                for n in range(2):
                    scores = lax.dot_general(
                        q_aug[n, rows, :], k_aug[n], (((1,), (1,)), ((), ())), preferred_element_type=F32
                    )
                    top = jnp.max(scores, axis=1, keepdims=True)
                    terms = jnp.exp2((scores - top) * SCORE_FACTOR).astype(BF)
                    got = jnp.dot(terms, v_aug[n], preferred_element_type=F32)
                    mixed.append(got / pltpu.roll(got, 64, 1))
                both = jnp.where(low, mixed[0], mixed[1]).astype(BF)
                attended[pl.ds(i * 4, 4)] = both.reshape(4, 64, 128)
                return carry

            lax.fori_loop(start, stop, block, 0)

    started = send_phase(0)
    attend(0, 1)
    for _, _, copy in started:
        copy.wait_recv()
    started = send_phase(1)
    attend(1, 3)
    for _, _, copy in started:
        copy.wait_recv()
    started = send_phase(2)
    for piece in pieces:
        share(piece, 0, area(piece, order[piece][:2]))
    attend(3, 8)

    columns = pl.ds(pl.multiple_of((me.h * 2 + pair) * 128, 128), 128)
    slot = lax.rem(prompt, 3)
    lands_here = me.h == me.z

    @pl.when(busy)
    def _():
        def post(i, carry):
            to = lax.rem(me.s + i, 32)
            remote(
                attended.at[to], joined.at[slot, :, columns], mix_send, mix_recv, (to, me.z)
            ).start()
            return carry

        lax.fori_loop(1, 32, post, 0)

        @pl.when(lands_here)
        def _():
            keep = pltpu.make_async_copy(attended.at[me.s], joined.at[slot, :, columns], mix_own)
            keep.start()
            keep.wait()

        @pl.when(jnp.logical_not(lands_here))
        def _():
            remote(
                attended.at[me.s], joined.at[slot, :, columns], mix_send, mix_recv, (me.s, me.z)
            ).start()

    for piece, d, copy in started:
        copy.wait_recv()
        dims = order[piece]
        share(piece, d, area(piece, dims[:2], (dims[2], 4 - d)))

    mine_too = jnp.logical_and(busy, lands_here)

    @pl.when(mine_too)
    def _():
        part = attended.at[pl.ds(0, 23)]
        pltpu.make_async_copy(part, part, mix_recv).wait()

    @pl.when(jnp.logical_not(mine_too))
    def _():
        part = attended.at[pl.ds(0, 24)]
        pltpu.make_async_copy(part, part, mix_recv).wait()

    for copy in shares:
        copy.wait_recv()

    x_rows = x_ref[pl.ds(me.h * 3, 3)].reshape(192, 1024).astype(F32)
    mixed = joined[...].reshape(192, 1024)
    sums = jnp.concatenate(
        [jnp.dot(mixed, w_out[n].reshape(1024, 512), preferred_element_type=F32) for n in range(2)], axis=1
    )
    normed = normalize(sums + x_rows, gain_ref[0:1], bias_ref[0:1]).astype(BF)
    for n in range(2):
        for k in range(4):
            w = w_in[n, :, :, :, :, :, k * 512 : (k + 1) * 512].reshape(1024, 512)
            units = jnp.dot(normed, w, preferred_element_type=F32)
            units = 0.5 * units * (1.0 + lax.erf(units * (2.0**-0.5)))
            hidden[n * 4 + k] = units.astype(BF)
    total = normed.astype(F32)
    for k in range(8):
        w = w_down[k // 2, k % 2].reshape(512, 1024)
        total = total + jnp.dot(hidden[k], w, preferred_element_type=F32)
    final = normalize(total, gain_ref[1:2], bias_ref[1:2]).astype(BF)
    for n in range(4):
        result[n] = final[:, n * 256 : (n + 1) * 256].reshape(3, 64, 256)
    rows = pl.ds(me.h * 3, 3)
    hidden_ref[rows] = result[me.h]
    last = []
    for d in range(1, 4):
        to = lax.rem(me.h + d, 4)
        copy = remote(result.at[to], hidden_ref.at[rows], last_send.at[d - 1], last_recv.at[d - 1], (me.s, to))
        copy.start()
        last.append(copy)

    @pl.when(jnp.logical_and(busy, lands_here))
    def _():
        part = attended.at[pl.ds(0, 31)]
        pltpu.make_async_copy(part, part, mix_send).wait()

    @pl.when(jnp.logical_and(busy, jnp.logical_not(lands_here)))
    def _():
        pltpu.make_async_copy(attended, attended, mix_send).wait()

    for copy in swaps + pending:
        copy.wait_send()
    for copy in last:
        copy.wait()


def layer(qkv, x, lengths, w_attn_out, w_in, w_down, ln_gain, ln_bias):
    vmem = pl.BlockSpec(memory_space=pltpu.VMEM)
    dma = pltpu.SemaphoreType.DMA
    return pl.pallas_call(
        layer_kernel,
        out_shape=jax.ShapeDtypeStruct((12, 64, 256), BF),
        in_specs=[vmem, vmem, pl.BlockSpec(memory_space=pltpu.SMEM)] + [vmem] * 5,
        out_specs=vmem,
        scratch_shapes=[
            pltpu.VMEM((8, 2048), F32),
            pltpu.VMEM((8, 512), F32),
            pltpu.VMEM((2, 4, 2, 4, 2, 16, 2048), BF),
            pltpu.VMEM((2, 4, 2, 4, 2, 16, 512), BF),
            pltpu.VMEM((4, 2, 4, 2, 2, 32, 1024), BF),
            pltpu.VMEM((2, 2048, 128), BF),
            pltpu.VMEM((2, 2048, 128), BF),
            pltpu.VMEM((2, 2048, 128), BF),
            pltpu.VMEM((32, 64, 128), BF),
            pltpu.VMEM((3, 64, 1024), BF),
            pltpu.VMEM((8, 192, 512), BF),
            pltpu.VMEM((4, 3, 64, 256), BF),
            dma((2,)),
            dma((2,)),
            dma((5, 3, 3)),
            dma((5, 3, 3)),
            dma((5, 4)),
            dma((5, 4)),
            dma,
            dma,
            dma,
            dma((3,)),
            dma((3,)),
        ],
        compiler_params=pltpu.CompilerParams(collective_id=1, has_side_effects=True, vmem_limit_bytes=58 << 20),
    )(qkv, x, lengths, w_attn_out, w_in, w_down, ln_gain, ln_bias)


def per_device(hidden_in, lengths, w_qkv, w_attn_out, w_in, w_down, ln_gain, ln_bias):
    key_cache, value_cache, qkv = project(hidden_in, w_qkv, lengths)
    hidden_out = layer(qkv, hidden_in, lengths, w_attn_out, w_in, w_down, ln_gain, ln_bias)
    return (hidden_out, key_cache, value_cache)


def solution(mesh):
    rows = P(("seq", "head"), None)
    in_specs = (P(None, "seq", None), P(), rows, rows, rows, rows, P(), P())
    out_specs = (P(None, "seq", "head"),) * 3
    return jax.shard_map(per_device, mesh=mesh, in_specs=in_specs, out_specs=out_specs, check_vma=False)
```

```python
import math

import jax
import jax.numpy as jnp
from jax import lax
from jax.experimental import pallas as pl
from jax.experimental.pallas import tpu as pltpu
from jax.sharding import PartitionSpec as P

MESH = pl.DeviceIdType.MESH
BF = jnp.bfloat16
F32 = jnp.float32
EPSILON = 1e-05
SCORE_FACTOR = 64 ** (-0.5) * math.log2(math.e)
DEAD = -1e30
IN_CUT = 1536
DOWN_CUT = 768


class Place:
    def __init__(self):
        self.s = lax.axis_index("seq")
        self.h = lax.axis_index("head")
        self.z = self.s // 8
        self.xl = lax.rem(self.s // 4, 2)
        self.y = lax.rem(self.s, 4)
        self.xh = self.h // 2
        self.c = lax.rem(self.h, 2)
        self.x = self.xh * 2 + self.xl

    def peer(self, dim, d):
        x, y, z = self.x, self.y, self.z
        if dim == "x":
            x = lax.rem(x + d, 4)
        elif dim == "y":
            y = lax.rem(y + d, 4)
        else:
            z = lax.rem(z + d, 4)
        return (z * 8 + lax.rem(x, 2) * 4 + y, (x // 2) * 2 + self.c)

    def sibling(self):
        return (self.s, self.xh * 2 + 1 - self.c)


def duty(s):
    z, xl, y = s // 8, lax.rem(s // 4, 2), lax.rem(s, 4)
    r = lax.rem(y + z, 4)
    return z * 3 + r, xl, r < 3


def remote(src, dst, send, recv, device):
    return pltpu.make_async_remote_copy(
        src_ref=src, dst_ref=dst, send_sem=send, recv_sem=recv, device_id=device, device_id_type=MESH
    )


def greet(barrier, device):
    pl.semaphore_signal(barrier, inc=1, device_id=device, device_id_type=MESH)


def normalize(rows, gain, shift):
    average = jnp.mean(rows, axis=1, keepdims=True)
    spread = jnp.mean(rows * rows, axis=1, keepdims=True) - average * average
    return (rows - average) * lax.rsqrt(spread + EPSILON) * gain + shift


def layer_kernel(
    x_hbm, len_ref, qkv_hbm, out_hbm, in_hbm, down_hbm, gain_ref, bias_ref, hidden_hbm, kc_hbm, vc_hbm,
    x_ref, qkv_f32, out_f32, in_f32, down_f32, other, qkv_half, in_half, out_half,
    slab, w_qkv, w_in, w_out, w_down, outbox, inbox, q_aug, k_aug, v_aug, attended, joined, hidden, result,
    caches, load_sem, swap_send, swap_recv, one_send, one_recv, two_send, two_recv, three_send, three_recv,
    box_own, box_send, box_recv, cache_sem, ring_send, ring_recv, last_ring_send, last_ring_recv,
    share_send, share_recv, mix_send, mix_recv, mix_own, back_send, back_recv, back_own,
):
    me = Place()
    prompt, pair, busy = duty(me.s)
    sibling = me.sibling()
    loads = [
        pltpu.make_async_copy(source, target, load_sem.at[n])
        for n, (source, target) in enumerate(
            (
                (qkv_hbm, qkv_f32), (out_hbm, out_f32), (in_hbm, in_f32), (down_hbm, down_f32), (x_hbm, x_ref),
            )
        )
    ]
    for copy in loads:
        copy.start()
    barrier = pltpu.get_barrier_semaphore()

    def greet_seq(i, carry):
        greet(barrier, (lax.rem(me.s + i, 32), me.h))
        return carry

    greet(barrier, sibling)
    for xl in range(2):
        greet(barrier, (me.z * 8 + xl * 4 + me.y, (1 - me.xh) * 2 + me.c))
    lax.fori_loop(1, 32, greet_seq, 0)

    loads[0].wait()
    for k in range(2):
        for t in range(3):
            at = pl.multiple_of(t * 1024 + (2 * k + 1 - me.c) * 256, 256)
            other[:, k * 768 + t * 256 : k * 768 + (t + 1) * 256] = qkv_f32[:, pl.ds(at, 256)]
    loads[1].wait()
    loads[2].wait()
    there = 1 - me.c
    swaps = [
        remote(other, qkv_half, swap_send.at[0], swap_recv.at[0], sibling),
        remote(
            out_f32.at[:, pl.ds(pl.multiple_of(there * 512, 512), 512)],
            out_half, swap_send.at[1], swap_recv.at[1], sibling,
        ),
        remote(
            in_f32.at[:, pl.ds(pl.multiple_of(there * 2048, 2048), 2048)],
            in_half, swap_send.at[2], swap_recv.at[2], sibling,
        ),
    ]
    pl.semaphore_wait(barrier, 34)
    for copy in swaps:
        copy.start()
    loads[3].wait()
    w_down[me.z, me.xl, me.y, me.xh, me.c] = down_f32[...].astype(BF)
    first = me.c == 0

    def stack(mine, sent):
        rows = jnp.concatenate([jnp.where(first, mine, sent), jnp.where(first, sent, mine)], axis=0)
        return rows.astype(BF)

    swaps[0].wait_recv()
    for k in range(2):
        for t in range(3):
            at = pl.multiple_of(t * 1024 + (2 * k + me.c) * 256, 256)
            cols = slice(k * 768 + t * 256, k * 768 + (t + 1) * 256)
            slab[k, :, t * 256 : (t + 1) * 256] = stack(qkv_f32[:, pl.ds(at, 256)], qkv_half[:, cols])
    w_qkv[me.z, me.xl, me.y, me.xh] = slab[me.xh]
    pending = []
    one = []
    for d in (1, 3, 2):
        target = me.peer("x", d)
        copy = remote(
            slab.at[target[1] // 2], w_qkv.at[me.z, me.xl, me.y, me.xh], one_send.at[d - 1], one_recv.at[d - 1], target
        )
        copy.start()
        one.append(copy)
    pending += one

    for n, (source, half, width, target) in enumerate(
        ((out_f32, out_half, 512, w_out), (in_f32, in_half, 2048, w_in))
    ):
        swaps[n + 1].wait_recv()
        mine = source[:, pl.ds(pl.multiple_of(me.c * width, width), width)]
        target[me.c, me.z, me.xl, me.y, me.xh] = stack(mine, half[...])

    one_c = pl.ds(me.c, 1)

    def region(piece, zs, xls, ys, xhs):
        rows16, rows32 = pl.ds(0, 16), pl.ds(0, 32)
        if piece == 0:
            return w_in.at[one_c, zs, xls, ys, xhs, rows16, pl.ds(0, IN_CUT)]
        if piece == 1:
            return w_out.at[one_c, zs, xls, ys, xhs, rows16, pl.ds(0, 512)]
        if piece == 2:
            return w_in.at[one_c, zs, xls, ys, xhs, rows16, pl.ds(IN_CUT, 2048 - IN_CUT)]
        if piece == 3:
            return w_down.at[zs, xls, ys, xhs, one_c, rows32, pl.ds(DOWN_CUT, 1024 - DOWN_CUT)]
        return w_down.at[zs, xls, ys, xhs, one_c, rows32, pl.ds(0, DOWN_CUT)]

    order = {0: "xyz", 1: "yzx", 2: "yzx", 3: "yzx", 4: "zxy"}
    pieces = (1, 0, 2, 4, 3)

    def area(piece, done, at=None, half=None):
        x, y, z = me.x, me.y, me.z
        if at is not None:
            dim, d = at
            x = lax.rem(x + d, 4) if dim == "x" else x
            y = lax.rem(y + d, 4) if dim == "y" else y
            z = lax.rem(z + d, 4) if dim == "z" else z
        zs = pl.ds(0, 4) if "z" in done else pl.ds(z, 1)
        ys = pl.ds(0, 4) if "y" in done else pl.ds(y, 1)
        xls = pl.ds(0, 2) if "x" in done else pl.ds(lax.rem(x, 2), 1)
        xhs = pl.ds(0, 2) if "x" in done else pl.ds(x // 2, 1)
        if half is not None:
            if "z" in done:
                zs = pl.ds(half * 2, 2)
            else:
                ys = pl.ds(half * 2, 2)
        return region(piece, zs, xls, ys, xhs)

    def send_phase(phase):
        started = []
        for piece in pieces:
            dims = order[piece]
            part = area(piece, dims[:phase])
            for d in (1, 3, 2):
                copy = remote(
                    part, part, ring_send.at[piece, phase, d - 1], ring_recv.at[piece, phase, d - 1],
                    me.peer(dims[phase], d),
                )
                copy.start()
                started.append(copy)
                pending.append(copy)
        return started

    shares = []

    def share(piece, slot, part):
        copy = remote(part, part, share_send.at[piece, slot], share_recv.at[piece, slot], sibling)
        copy.start()
        shares.append(copy)
        pending.append(copy)

    def pass_on(piece, way, step):
        dims = order[piece]
        dim = dims[2]
        half = (step + way) % 2 if step < 2 else way
        back = 3 if way == 0 else 1
        at = None if step < 2 else (dim, back)
        part = area(piece, dims[:2], at, half)
        copy = remote(
            part, part, last_ring_send.at[piece, way, step], last_ring_recv.at[piece, way, step],
            me.peer(dim, 1 if way == 0 else 3),
        )
        copy.start()
        pending.append(copy)
        return copy

    def came(piece, way, step):
        dims = order[piece]
        half = (step + way) % 2 if step < 2 else way
        back = 3 if way == 0 else 1
        return area(piece, dims[:2], (dims[2], back if step < 2 else 2), half)

    rings = {}

    def ring_start(step):
        for piece in pieces:
            for way in range(2):
                rings[piece, way, step] = pass_on(piece, way, step)

    def ring_take(step, forward):
        for piece in pieces:
            for way in range(2):
                rings[piece, way, step].wait_recv()
                if forward:
                    rings[piece, way, 2] = pass_on(piece, way, 2)
                share(piece, 1 + way * 3 + step, came(piece, way, step))

    bulk_one = send_phase(0)
    for copy in one:
        copy.wait_recv()
    left, right = pl.ds(0, 384), pl.ds(384, 384)
    all2, all4, all16 = pl.ds(0, 2), pl.ds(0, 4), pl.ds(0, 16)
    zs, ys = pl.ds(me.z, 1), pl.ds(me.y, 1)
    two = []
    for d in (1, 3, 2):
        for k, (dim, cols) in enumerate((("y", left), ("z", right))):
            part = w_qkv.at[zs, all2, ys, all2, all16, cols]
            copy = remote(part, part, two_send.at[k, d - 1], two_recv.at[k, d - 1], me.peer(dim, d))
            copy.start()
            two.append(copy)
    pending += two
    for copy in bulk_one:
        copy.wait_recv()
    bulk_two = send_phase(1)
    for copy in two:
        copy.wait_recv()
    three = []
    for d in (1, 3, 2):
        for k, dim in enumerate(("z", "y")):
            if k == 0:
                part = w_qkv.at[zs, all2, all4, all2, all16, left]
            else:
                part = w_qkv.at[all4, all2, ys, all2, all16, right]
            copy = remote(part, part, three_send.at[k, d - 1], three_recv.at[k, d - 1], me.peer(dim, d))
            copy.start()
            three.append(copy)
    pending += three
    loads[4].wait()
    for copy in three:
        copy.wait_recv()

    for t in range(3):
        w = w_qkv[:, :, :, :, :, t * 256 : (t + 1) * 256].reshape(1024, 256)
        for g in range(2):
            rows = x_ref[g * 6 : (g + 1) * 6].reshape(384, 1024)
            got = jnp.dot(rows, w, preferred_element_type=F32)
            for q in range(6):
                p = g * 6 + q
                piece = got[q * 64 : (q + 1) * 64]
                if t > 0:
                    at = me.s * 64 + lax.broadcasted_iota(jnp.int32, (64, 256), 0)
                    piece = jnp.where(at < len_ref[p], piece, 0.0)
                piece = piece.astype(BF)
                if t > 0:
                    caches[t - 1, p] = piece
                outbox[p * 2, t] = piece[:, :128]
                outbox[p * 2 + 1, t] = piece[:, 128:]

    def post(i, carry):
        to = lax.rem(me.s + i, 32)
        their_prompt, their_pair, their_busy = duty(to)

        @pl.when(their_busy)
        def _():
            remote(
                outbox.at[their_prompt * 2 + their_pair], inbox.at[:, me.s], box_send, box_recv, (to, me.h)
            ).start()

        return carry

    lax.fori_loop(1, 32, post, 0)
    keeps = [
        pltpu.make_async_copy(caches.at[0], kc_hbm, cache_sem.at[0]),
        pltpu.make_async_copy(caches.at[1], vc_hbm, cache_sem.at[1]),
    ]
    for copy in keeps:
        copy.start()

    for copy in bulk_two:
        copy.wait_recv()
    ring_start(0)
    ring_start(1)
    for piece in pieces:
        share(piece, 0, area(piece, order[piece][:2]))

    @pl.when(busy)
    def _():
        keep = pltpu.make_async_copy(outbox.at[prompt * 2 + pair], inbox.at[:, me.s], box_own)
        keep.start()
        keep.wait()
        arrived = inbox.at[:, pl.ds(0, 31)]
        pltpu.make_async_copy(arrived, arrived, box_recv).wait()
        lane = lax.broadcasted_iota(jnp.int32, (2048, 128), 1)
        place = lax.broadcasted_iota(jnp.int32, (2048, 128), 0)
        bias = jnp.where(place < len_ref[prompt], 0.0, DEAD)
        q = inbox[0].reshape(2048, 128).astype(F32)
        k = inbox[1].reshape(2048, 128).astype(F32)
        v = inbox[2].reshape(2048, 128).astype(F32)
        for n in range(2):
            own = (lane // 64) == n
            mark = lane == (1 - n) * 64
            q_aug[n] = jnp.where(own, q, jnp.where(mark, 1.0, 0.0)).astype(BF)
            k_aug[n] = jnp.where(mark, bias, k).astype(BF)
            v_aug[n] = jnp.where(own, v, 1.0).astype(BF)

    low = lax.broadcasted_iota(jnp.int32, (256, 128), 1) < 64
    columns = pl.ds(pl.multiple_of((me.h * 2 + pair) * 128, 128), 128)
    slot = lax.rem(prompt, 3)
    lands_here = me.h == me.z

    def attend(start, stop):
        @pl.when(busy)
        def _():
            def block(i, carry):
                rows = pl.ds(pl.multiple_of(i * 256, 256), 256)
                mixed = []
                for n in range(2):
                    scores = lax.dot_general(
                        q_aug[n, rows, :], k_aug[n], (((1,), (1,)), ((), ())), preferred_element_type=F32
                    )
                    top = jnp.max(scores, axis=1, keepdims=True)
                    terms = jnp.exp2((scores - top) * SCORE_FACTOR).astype(BF)
                    got = jnp.dot(terms, v_aug[n], preferred_element_type=F32)
                    mixed.append(got / pltpu.roll(got, 64, 1))
                both = jnp.where(low, mixed[0], mixed[1]).astype(BF)
                attended[pl.ds(i * 4, 4)] = both.reshape(4, 64, 128)
                for k in range(4):
                    to = i * 4 + k
                    stays = jnp.logical_and(lands_here, to == me.s)

                    @pl.when(stays)
                    def _():
                        pltpu.make_async_copy(attended.at[to], joined.at[slot, :, columns], mix_own).start()

                    @pl.when(jnp.logical_not(stays))
                    def _():
                        remote(
                            attended.at[to], joined.at[slot, :, columns], mix_send, mix_recv, (to, me.z)
                        ).start()

                return carry

            lax.fori_loop(start, stop, block, 0)

    attend(0, 3)
    ring_take(0, True)
    attend(3, 8)
    ring_take(1, False)
    ring_take(2, False)
    mine_too = jnp.logical_and(busy, lands_here)

    @pl.when(mine_too)
    def _():
        pltpu.make_async_copy(attended.at[me.s], joined.at[slot, :, columns], mix_own).wait()
        part = attended.at[pl.ds(0, 23)]
        pltpu.make_async_copy(part, part, mix_recv).wait()

    @pl.when(jnp.logical_not(mine_too))
    def _():
        part = attended.at[pl.ds(0, 24)]
        pltpu.make_async_copy(part, part, mix_recv).wait()

    for copy in shares:
        copy.wait_recv()

    x_rows = x_ref[pl.ds(me.h * 3, 3)].reshape(192, 1024).astype(F32)
    mixed = joined[...].reshape(192, 1024)
    sums = jnp.concatenate(
        [jnp.dot(mixed, w_out[n].reshape(1024, 512), preferred_element_type=F32) for n in range(2)], axis=1
    )
    normed = normalize(sums + x_rows, gain_ref[0:1], bias_ref[0:1]).astype(BF)
    for n in range(2):
        for k in range(4):
            w = w_in[n, :, :, :, :, :, k * 512 : (k + 1) * 512].reshape(1024, 512)
            units = jnp.dot(normed, w, preferred_element_type=F32)
            units = 0.5 * units * (1.0 + lax.erf(units * (2.0**-0.5)))
            hidden[n * 4 + k] = units.astype(BF)
    total = normed.astype(F32)
    for k in range(8):
        w = w_down[k // 2, k % 2].reshape(512, 1024)
        total = total + jnp.dot(hidden[k], w, preferred_element_type=F32)
    final = normalize(total, gain_ref[1:2], bias_ref[1:2]).astype(BF)
    for n in range(4):
        result[n] = final[:, n * 256 : (n + 1) * 256].reshape(3, 64, 256)
    rows = pl.ds(me.h * 3, 3)
    own = pltpu.make_async_copy(result.at[me.h], hidden_hbm.at[rows], back_own)
    own.start()
    last = []
    for d in range(1, 4):
        to = lax.rem(me.h + d, 4)
        copy = remote(result.at[to], hidden_hbm.at[rows], back_send.at[d - 1], back_recv.at[d - 1], (me.s, to))
        copy.start()
        last.append(copy)

    @pl.when(busy)
    def _():
        gone = outbox.at[pl.ds(0, 23)]
        pltpu.make_async_copy(gone, gone, box_send).wait()

    @pl.when(jnp.logical_not(busy))
    def _():
        gone = outbox.at[pl.ds(0, 24)]
        pltpu.make_async_copy(gone, gone, box_send).wait()

    @pl.when(mine_too)
    def _():
        part = attended.at[pl.ds(0, 31)]
        pltpu.make_async_copy(part, part, mix_send).wait()

    @pl.when(jnp.logical_and(busy, jnp.logical_not(lands_here)))
    def _():
        pltpu.make_async_copy(attended, attended, mix_send).wait()

    for copy in swaps + pending:
        copy.wait_send()
    for copy in keeps:
        copy.wait()
    own.wait()
    for copy in last:
        copy.wait()


def layer(x, lengths, w_qkv, w_attn_out, w_in, w_down, ln_gain, ln_bias):
    vmem, hbm = pl.BlockSpec(memory_space=pltpu.VMEM), pl.BlockSpec(memory_space=pl.ANY)
    dma = pltpu.SemaphoreType.DMA
    return pl.pallas_call(
        layer_kernel,
        out_shape=(jax.ShapeDtypeStruct((12, 64, 256), BF),) * 3,
        in_specs=[hbm, pl.BlockSpec(memory_space=pltpu.SMEM), hbm, hbm, hbm, hbm, vmem, vmem],
        out_specs=(hbm,) * 3,
        scratch_shapes=[
            pltpu.VMEM((12, 64, 1024), BF),
            pltpu.VMEM((8, 3072), F32),
            pltpu.VMEM((8, 1024), F32),
            pltpu.VMEM((8, 4096), F32),
            pltpu.VMEM((32, 1024), F32),
            pltpu.VMEM((8, 1536), F32),
            pltpu.VMEM((8, 1536), F32),
            pltpu.VMEM((8, 2048), F32),
            pltpu.VMEM((8, 512), F32),
            pltpu.VMEM((2, 16, 768), BF),
            pltpu.VMEM((4, 2, 4, 2, 16, 768), BF),
            pltpu.VMEM((2, 4, 2, 4, 2, 16, 2048), BF),
            pltpu.VMEM((2, 4, 2, 4, 2, 16, 512), BF),
            pltpu.VMEM((4, 2, 4, 2, 2, 32, 1024), BF),
            pltpu.VMEM((24, 3, 64, 128), BF),
            pltpu.VMEM((3, 32, 64, 128), BF),
            pltpu.VMEM((2, 2048, 128), BF),
            pltpu.VMEM((2, 2048, 128), BF),
            pltpu.VMEM((2, 2048, 128), BF),
            pltpu.VMEM((32, 64, 128), BF),
            pltpu.VMEM((3, 64, 1024), BF),
            pltpu.VMEM((8, 192, 512), BF),
            pltpu.VMEM((4, 3, 64, 256), BF),
            pltpu.VMEM((2, 12, 64, 256), BF),
            dma((5,)),
            dma((3,)),
            dma((3,)),
            dma((3,)),
            dma((3,)),
            dma((2, 3)),
            dma((2, 3)),
            dma((2, 3)),
            dma((2, 3)),
            dma,
            dma,
            dma,
            dma((2,)),
            dma((5, 2, 3)),
            dma((5, 2, 3)),
            dma((5, 2, 3)),
            dma((5, 2, 3)),
            dma((5, 7)),
            dma((5, 7)),
            dma,
            dma,
            dma,
            dma((3,)),
            dma((3,)),
            dma,
        ],
        compiler_params=pltpu.CompilerParams(collective_id=0, has_side_effects=True, vmem_limit_bytes=58 << 20),
    )(x, lengths, w_qkv, w_attn_out, w_in, w_down, ln_gain, ln_bias)


def per_device(hidden_in, lengths, w_qkv, w_attn_out, w_in, w_down, ln_gain, ln_bias):
    return layer(hidden_in, lengths, w_qkv, w_attn_out, w_in, w_down, ln_gain, ln_bias)


def solution(mesh):
    rows = P(("seq", "head"), None)
    in_specs = (P(None, "seq", None), P(), rows, rows, rows, rows, P(), P())
    out_specs = (P(None, "seq", "head"),) * 3
    return jax.shard_map(per_device, mesh=mesh, in_specs=in_specs, out_specs=out_specs, check_vma=False)
```

```python
import math

import jax
import jax.numpy as jnp
from jax import lax
from jax.experimental import pallas as pl
from jax.experimental.pallas import tpu as pltpu
from jax.sharding import PartitionSpec as P

MESH = pl.DeviceIdType.MESH
BF = jnp.bfloat16
F32 = jnp.float32
EPSILON = 1e-05
SCORE_FACTOR = 64 ** (-0.5) * math.log2(math.e)
DEAD = -1e30
IN_X, IN_Z = 384, 768
DOWN_X, DOWN_Z = 512, 256


class Place:
    def __init__(self):
        self.s = lax.axis_index("seq")
        self.h = lax.axis_index("head")
        self.z = self.s // 8
        self.xl = lax.rem(self.s // 4, 2)
        self.y = lax.rem(self.s, 4)
        self.xh = self.h // 2
        self.c = lax.rem(self.h, 2)
        self.x = self.xh * 2 + self.xl

    def peer(self, dim, d):
        x, y, z = self.x, self.y, self.z
        if dim == "x":
            x = lax.rem(x + d, 4)
        elif dim == "y":
            y = lax.rem(y + d, 4)
        else:
            z = lax.rem(z + d, 4)
        return (z * 8 + lax.rem(x, 2) * 4 + y, (x // 2) * 2 + self.c)

    def sibling(self):
        return (self.s, self.xh * 2 + 1 - self.c)


def duty(s):
    z, xl, y = s // 8, lax.rem(s // 4, 2), lax.rem(s, 4)
    r = lax.rem(y + z, 4)
    return z * 3 + r, xl, r < 3


def remote(src, dst, send, recv, device):
    return pltpu.make_async_remote_copy(
        src_ref=src, dst_ref=dst, send_sem=send, recv_sem=recv, device_id=device, device_id_type=MESH
    )


class Ring:
    def __init__(self, me, view, dim, send, recv):
        self.me, self.view, self.dim, self.send, self.recv = me, view, dim, send, recv
        self.copies = {}

    def half(self, way, step):
        return (step + way) % 2 if step < 2 else way

    def go(self, way, step):
        behind = 3 if way == 0 else 1
        part = self.view(0 if step < 2 else behind, self.half(way, step))
        copy = remote(
            part, part, self.send(way, step), self.recv(way, step), self.me.peer(self.dim, 1 if way == 0 else 3)
        )
        copy.start()
        self.copies[way, step] = copy

    def came(self, way, step):
        behind = 3 if way == 0 else 1
        return self.view(behind if step < 2 else 2, self.half(way, step))


def greet(barrier, device):
    pl.semaphore_signal(barrier, inc=1, device_id=device, device_id_type=MESH)


def normalize(rows, gain, shift):
    average = jnp.mean(rows, axis=1, keepdims=True)
    spread = jnp.mean(rows * rows, axis=1, keepdims=True) - average * average
    return (rows - average) * lax.rsqrt(spread + EPSILON) * gain + shift


def layer_kernel(
    x_hbm, len_ref, qkv_hbm, out_hbm, in_hbm, down_hbm, gain_ref, bias_ref, hidden_hbm, kc_hbm, vc_hbm,
    x_ref, qkv_f32, out_f32, in_f32, down_f32, other, qkv_half, in_half, out_half,
    slab, w_qkv, w_in, w_out, w_down, outbox, inbox, q_aug, k_aug, v_aug, attended, joined, hidden, result,
    caches, load_sem, swap_send, swap_recv, one_send, one_recv, two_send, two_recv, three_send, three_recv,
    box_own, box_send, box_recv, cache_sem, first_send, first_recv, ring_send, ring_recv,
    share_send, share_recv, mix_send, mix_recv, mix_own, back_send, back_recv, back_own,
):
    me = Place()
    prompt, pair, busy = duty(me.s)
    sibling = me.sibling()
    loads = [
        pltpu.make_async_copy(source, target, load_sem.at[n])
        for n, (source, target) in enumerate(
            (
                (qkv_hbm, qkv_f32), (out_hbm, out_f32), (in_hbm, in_f32), (down_hbm, down_f32), (x_hbm, x_ref),
            )
        )
    ]
    for copy in loads:
        copy.start()
    barrier = pltpu.get_barrier_semaphore()

    def greet_seq(i, carry):
        greet(barrier, (lax.rem(me.s + i, 32), me.h))
        return carry

    greet(barrier, sibling)
    for xl in range(2):
        greet(barrier, (me.z * 8 + xl * 4 + me.y, (1 - me.xh) * 2 + me.c))
    lax.fori_loop(1, 32, greet_seq, 0)

    loads[0].wait()
    for k in range(2):
        for t in range(3):
            at = pl.multiple_of(t * 1024 + (2 * k + 1 - me.c) * 256, 256)
            other[:, k * 768 + t * 256 : k * 768 + (t + 1) * 256] = qkv_f32[:, pl.ds(at, 256)]
    loads[1].wait()
    loads[2].wait()
    there = 1 - me.c
    swaps = [
        remote(other, qkv_half, swap_send.at[0], swap_recv.at[0], sibling),
        remote(
            out_f32.at[:, pl.ds(pl.multiple_of(there * 512, 512), 512)],
            out_half, swap_send.at[1], swap_recv.at[1], sibling,
        ),
        remote(
            in_f32.at[:, pl.ds(pl.multiple_of(there * 2048, 2048), 2048)],
            in_half, swap_send.at[2], swap_recv.at[2], sibling,
        ),
    ]
    pl.semaphore_wait(barrier, 34)
    for copy in swaps:
        copy.start()
    loads[3].wait()
    w_down[me.z, me.xl, me.y, me.xh, me.c] = down_f32[...].astype(BF)
    first = me.c == 0

    def stack(mine, sent):
        rows = jnp.concatenate([jnp.where(first, mine, sent), jnp.where(first, sent, mine)], axis=0)
        return rows.astype(BF)

    swaps[0].wait_recv()
    for k in range(2):
        for t in range(3):
            at = pl.multiple_of(t * 1024 + (2 * k + me.c) * 256, 256)
            cols = slice(k * 768 + t * 256, k * 768 + (t + 1) * 256)
            slab[k, :, t * 256 : (t + 1) * 256] = stack(qkv_f32[:, pl.ds(at, 256)], qkv_half[:, cols])
    w_qkv[me.z, me.xl, me.y, me.xh] = slab[me.xh]
    pending = []
    one = []
    for d in (1, 3, 2):
        target = me.peer("x", d)
        copy = remote(
            slab.at[target[1] // 2], w_qkv.at[me.z, me.xl, me.y, me.xh], one_send.at[d - 1], one_recv.at[d - 1], target
        )
        copy.start()
        one.append(copy)
    pending += one

    for n, (source, half, width, target) in enumerate(
        ((out_f32, out_half, 512, w_out), (in_f32, in_half, 2048, w_in))
    ):
        swaps[n + 1].wait_recv()
        mine = source[:, pl.ds(pl.multiple_of(me.c * width, width), width)]
        target[me.c, me.z, me.xl, me.y, me.xh] = stack(mine, half[...])

    one_c = pl.ds(me.c, 1)

    def region(piece, zs, xls, ys, xhs):
        rows16, rows32 = pl.ds(0, 16), pl.ds(0, 32)
        if piece == 0:
            return w_out.at[one_c, zs, xls, ys, xhs, rows16, pl.ds(0, 512)]
        start, stop = cuts[piece]
        if piece < 4:
            return w_in.at[one_c, zs, xls, ys, xhs, rows16, pl.ds(start, stop - start)]
        return w_down.at[zs, xls, ys, xhs, one_c, rows32, pl.ds(start, stop - start)]

    cuts = {
        1: (0, IN_X), 2: (IN_X, IN_X + IN_Z), 3: (IN_X + IN_Z, 2048),
        4: (0, DOWN_X), 5: (DOWN_X, DOWN_X + DOWN_Z), 6: (DOWN_X + DOWN_Z, 1024),
    }
    order = {0: "yzx", 1: "yzx", 2: "xyz", 3: "zxy", 4: "yzx", 5: "xyz", 6: "zxy"}
    early, late = (0, 1, 2, 3), (4, 5, 6)
    pieces = early + late

    def area(piece, done, at=None, half=None):
        x, y, z = me.x, me.y, me.z
        if at is not None:
            dim, d = at
            x = lax.rem(x + d, 4) if dim == "x" else x
            y = lax.rem(y + d, 4) if dim == "y" else y
            z = lax.rem(z + d, 4) if dim == "z" else z
        zs = pl.ds(0, 4) if "z" in done else pl.ds(z, 1)
        ys = pl.ds(0, 4) if "y" in done else pl.ds(y, 1)
        xls = pl.ds(0, 2) if "x" in done else pl.ds(lax.rem(x, 2), 1)
        xhs = pl.ds(0, 2) if "x" in done else pl.ds(x // 2, 1)
        if half is not None:
            if "z" in done:
                zs = pl.ds(half * 2, 2)
            elif "y" in done:
                ys = pl.ds(half * 2, 2)
            else:
                xls = pl.ds(half, 1)
        return region(piece, zs, xls, ys, xhs)

    def send_first():
        started = []
        for piece in pieces:
            part = area(piece, "")
            for d in (1, 3, 2):
                copy = remote(
                    part, part, first_send.at[piece, d - 1], first_recv.at[piece, d - 1], me.peer(order[piece][0], d)
                )
                copy.start()
                started.append(copy)
                pending.append(copy)
        return started

    shares = {}

    def share(piece, slot, part):
        copy = remote(part, part, share_send.at[piece, slot], share_recv.at[piece, slot], sibling)
        copy.start()
        shares[piece, slot] = copy
        pending.append(copy)

    rings = {}
    for piece in pieces:
        for phase in (1, 2):
            dims = order[piece]
            rings[piece, phase] = Ring(
                me,
                lambda d, half, piece=piece, dims=dims, phase=phase: area(piece, dims[:phase], (dims[phase], d), half),
                dims[phase],
                lambda way, step, piece=piece, phase=phase: ring_send.at[piece, phase - 1, way, step],
                lambda way, step, piece=piece, phase=phase: ring_recv.at[piece, phase - 1, way, step],
            )

    def start(which, step):
        for ring in which:
            for way in range(2):
                ring.go(way, step)

    def take(which, step):
        for ring in which:
            for way in range(2):
                ring.copies[way, step].wait_recv()
                if step == 0:
                    ring.go(way, 2)

    def ring_start(group, step):
        start([rings[piece, 2] for piece in group], step)

    def ring_take(group, step):
        for piece in group:
            ring = rings[piece, 2]
            take([ring], step)
            for way in range(2):
                share(piece, 1 + way * 3 + step, ring.came(way, step))

    bulk_one = send_first()
    for copy in one:
        copy.wait_recv()
    left, right = pl.ds(0, 384), pl.ds(384, 384)
    all2, all4, all16 = pl.ds(0, 2), pl.ds(0, 4), pl.ds(0, 16)
    zs, ys = pl.ds(me.z, 1), pl.ds(me.y, 1)
    two = []
    for d in (1, 3, 2):
        for k, (dim, cols) in enumerate((("y", left), ("z", right))):
            part = w_qkv.at[zs, all2, ys, all2, all16, cols]
            copy = remote(part, part, two_send.at[k, d - 1], two_recv.at[k, d - 1], me.peer(dim, d))
            copy.start()
            two.append(copy)
    pending += two
    for copy in bulk_one:
        copy.wait_recv()
    middle = [rings[piece, 1] for piece in pieces]
    start(middle, 0)
    start(middle, 1)
    for copy in two:
        copy.wait_recv()

    def view_left(d, half):
        return w_qkv.at[pl.ds(lax.rem(me.z + d, 4), 1), all2, pl.ds(half * 2, 2), all2, all16, left]

    def view_right(d, half):
        return w_qkv.at[pl.ds(half * 2, 2), all2, pl.ds(lax.rem(me.y + d, 4), 1), all2, all16, right]

    three = [
        Ring(
            me, view, dim,
            lambda way, step, k=k: three_send.at[k, way, step],
            lambda way, step, k=k: three_recv.at[k, way, step],
        )
        for k, (view, dim) in enumerate(((view_left, "z"), (view_right, "y")))
    ]
    start(three, 0)
    start(three, 1)
    take(three, 0)
    take(middle, 0)
    loads[4].wait()
    take(three, 1)
    take(three, 2)

    for t in range(3):
        w = w_qkv[:, :, :, :, :, t * 256 : (t + 1) * 256].reshape(1024, 256)
        for g in range(2):
            rows = x_ref[g * 6 : (g + 1) * 6].reshape(384, 1024)
            got = jnp.dot(rows, w, preferred_element_type=F32)
            for q in range(6):
                p = g * 6 + q
                piece = got[q * 64 : (q + 1) * 64]
                if t > 0:
                    at = me.s * 64 + lax.broadcasted_iota(jnp.int32, (64, 256), 0)
                    piece = jnp.where(at < len_ref[p], piece, 0.0)
                piece = piece.astype(BF)
                if t > 0:
                    caches[t - 1, p] = piece
                outbox[p * 2, t] = piece[:, :128]
                outbox[p * 2 + 1, t] = piece[:, 128:]

    def post(i, carry):
        to = lax.rem(me.s + i, 32)
        their_prompt, their_pair, their_busy = duty(to)

        @pl.when(their_busy)
        def _():
            remote(
                outbox.at[their_prompt * 2 + their_pair], inbox.at[:, me.s], box_send, box_recv, (to, me.h)
            ).start()

        return carry

    lax.fori_loop(1, 32, post, 0)
    keeps = [
        pltpu.make_async_copy(caches.at[0], kc_hbm, cache_sem.at[0]),
        pltpu.make_async_copy(caches.at[1], vc_hbm, cache_sem.at[1]),
    ]
    for copy in keeps:
        copy.start()

    take(middle, 1)
    take(middle, 2)
    ring_start(early, 0)
    ring_start(early, 1)
    for piece in pieces:
        share(piece, 0, area(piece, order[piece][:2]))
    ring_take(early, 0)
    ring_start(late, 0)
    ring_take(early, 1)
    ring_start(late, 1)

    @pl.when(busy)
    def _():
        keep = pltpu.make_async_copy(outbox.at[prompt * 2 + pair], inbox.at[:, me.s], box_own)
        keep.start()
        keep.wait()
        arrived = inbox.at[:, pl.ds(0, 31)]
        pltpu.make_async_copy(arrived, arrived, box_recv).wait()
        lane = lax.broadcasted_iota(jnp.int32, (2048, 128), 1)
        place = lax.broadcasted_iota(jnp.int32, (2048, 128), 0)
        bias = jnp.where(place < len_ref[prompt], 0.0, DEAD)
        q = inbox[0].reshape(2048, 128).astype(F32)
        k = inbox[1].reshape(2048, 128).astype(F32)
        v = inbox[2].reshape(2048, 128).astype(F32)
        for n in range(2):
            own = (lane // 64) == n
            mark = lane == (1 - n) * 64
            q_aug[n] = jnp.where(own, q, jnp.where(mark, 1.0, 0.0)).astype(BF)
            k_aug[n] = jnp.where(mark, bias, k).astype(BF)
            v_aug[n] = jnp.where(own, v, 1.0).astype(BF)

    low = lax.broadcasted_iota(jnp.int32, (256, 128), 1) < 64
    columns = pl.ds(pl.multiple_of((me.h * 2 + pair) * 128, 128), 128)
    slot = lax.rem(prompt, 3)
    lands_here = me.h == me.z

    def attend(start, stop):
        @pl.when(busy)
        def _():
            def block(i, carry):
                rows = pl.ds(pl.multiple_of(i * 256, 256), 256)
                mixed = []
                for n in range(2):
                    scores = lax.dot_general(
                        q_aug[n, rows, :], k_aug[n], (((1,), (1,)), ((), ())), preferred_element_type=F32
                    )
                    top = jnp.max(scores, axis=1, keepdims=True)
                    terms = jnp.exp2((scores - top) * SCORE_FACTOR).astype(BF)
                    got = jnp.dot(terms, v_aug[n], preferred_element_type=F32)
                    mixed.append(got / pltpu.roll(got, 64, 1))
                both = jnp.where(low, mixed[0], mixed[1]).astype(BF)
                attended[pl.ds(i * 4, 4)] = both.reshape(4, 64, 128)
                for k in range(4):
                    to = i * 4 + k
                    stays = jnp.logical_and(lands_here, to == me.s)

                    @pl.when(stays)
                    def _():
                        pltpu.make_async_copy(attended.at[to], joined.at[slot, :, columns], mix_own).start()

                    @pl.when(jnp.logical_not(stays))
                    def _():
                        remote(
                            attended.at[to], joined.at[slot, :, columns], mix_send, mix_recv, (to, me.z)
                        ).start()

                return carry

            lax.fori_loop(start, stop, block, 0)

    attend(0, 2)
    ring_take(early, 2)
    attend(2, 6)
    ring_take(late, 0)
    attend(6, 8)
    ring_take(late, 1)
    mine_too = jnp.logical_and(busy, lands_here)

    @pl.when(mine_too)
    def _():
        pltpu.make_async_copy(attended.at[me.s], joined.at[slot, :, columns], mix_own).wait()
        part = attended.at[pl.ds(0, 23)]
        pltpu.make_async_copy(part, part, mix_recv).wait()

    @pl.when(jnp.logical_not(mine_too))
    def _():
        part = attended.at[pl.ds(0, 24)]
        pltpu.make_async_copy(part, part, mix_recv).wait()

    for key, copy in shares.items():
        if key[0] in early:
            copy.wait_recv()

    x_rows = x_ref[pl.ds(me.h * 3, 3)].reshape(192, 1024).astype(F32)
    mixed = joined[...].reshape(192, 1024)
    sums = jnp.concatenate(
        [jnp.dot(mixed, w_out[n].reshape(1024, 512), preferred_element_type=F32) for n in range(2)], axis=1
    )
    normed = normalize(sums + x_rows, gain_ref[0:1], bias_ref[0:1]).astype(BF)
    for n in range(2):
        for k in range(4):
            w = w_in[n, :, :, :, :, :, k * 512 : (k + 1) * 512].reshape(1024, 512)
            units = jnp.dot(normed, w, preferred_element_type=F32)
            units = 0.5 * units * (1.0 + lax.erf(units * (2.0**-0.5)))
            hidden[n * 4 + k] = units.astype(BF)
    ring_take(late, 2)
    for key, copy in shares.items():
        if key[0] in late:
            copy.wait_recv()
    total = normed.astype(F32)
    for k in range(8):
        w = w_down[k // 2, k % 2].reshape(512, 1024)
        total = total + jnp.dot(hidden[k], w, preferred_element_type=F32)
    final = normalize(total, gain_ref[1:2], bias_ref[1:2]).astype(BF)
    for n in range(4):
        result[n] = final[:, n * 256 : (n + 1) * 256].reshape(3, 64, 256)
    rows = pl.ds(me.h * 3, 3)
    own = pltpu.make_async_copy(result.at[me.h], hidden_hbm.at[rows], back_own)
    own.start()
    last = []
    for d in range(1, 4):
        to = lax.rem(me.h + d, 4)
        copy = remote(result.at[to], hidden_hbm.at[rows], back_send.at[d - 1], back_recv.at[d - 1], (me.s, to))
        copy.start()
        last.append(copy)

    @pl.when(busy)
    def _():
        gone = outbox.at[pl.ds(0, 23)]
        pltpu.make_async_copy(gone, gone, box_send).wait()

    @pl.when(jnp.logical_not(busy))
    def _():
        gone = outbox.at[pl.ds(0, 24)]
        pltpu.make_async_copy(gone, gone, box_send).wait()

    @pl.when(mine_too)
    def _():
        part = attended.at[pl.ds(0, 31)]
        pltpu.make_async_copy(part, part, mix_send).wait()

    @pl.when(jnp.logical_and(busy, jnp.logical_not(lands_here)))
    def _():
        pltpu.make_async_copy(attended, attended, mix_send).wait()

    for ring in [*rings.values(), *three]:
        pending += ring.copies.values()
    for copy in swaps + pending:
        copy.wait_send()
    for copy in keeps:
        copy.wait()
    own.wait()
    for copy in last:
        copy.wait()


def layer(x, lengths, w_qkv, w_attn_out, w_in, w_down, ln_gain, ln_bias):
    vmem, free = pl.BlockSpec(memory_space=pltpu.VMEM), pl.BlockSpec(memory_space=pl.ANY)
    hbm = pl.BlockSpec(memory_space=pltpu.HBM)
    dma = pltpu.SemaphoreType.DMA
    return pl.pallas_call(
        layer_kernel,
        out_shape=(jax.ShapeDtypeStruct((12, 64, 256), BF),) * 3,
        in_specs=[hbm, pl.BlockSpec(memory_space=pltpu.SMEM), hbm, hbm, hbm, hbm, vmem, vmem],
        out_specs=(free,) * 3,
        scratch_shapes=[
            pltpu.VMEM((12, 64, 1024), BF),
            pltpu.VMEM((8, 3072), F32),
            pltpu.VMEM((8, 1024), F32),
            pltpu.VMEM((8, 4096), F32),
            pltpu.VMEM((32, 1024), F32),
            pltpu.VMEM((8, 1536), F32),
            pltpu.VMEM((8, 1536), F32),
            pltpu.VMEM((8, 2048), F32),
            pltpu.VMEM((8, 512), F32),
            pltpu.VMEM((2, 16, 768), BF),
            pltpu.VMEM((4, 2, 4, 2, 16, 768), BF),
            pltpu.VMEM((2, 4, 2, 4, 2, 16, 2048), BF),
            pltpu.VMEM((2, 4, 2, 4, 2, 16, 512), BF),
            pltpu.VMEM((4, 2, 4, 2, 2, 32, 1024), BF),
            pltpu.VMEM((24, 3, 64, 128), BF),
            pltpu.VMEM((3, 32, 64, 128), BF),
            pltpu.VMEM((2, 2048, 128), BF),
            pltpu.VMEM((2, 2048, 128), BF),
            pltpu.VMEM((2, 2048, 128), BF),
            pltpu.VMEM((32, 64, 128), BF),
            pltpu.VMEM((3, 64, 1024), BF),
            pltpu.VMEM((8, 192, 512), BF),
            pltpu.VMEM((4, 3, 64, 256), BF),
            pltpu.VMEM((2, 12, 64, 256), BF),
            dma((5,)),
            dma((3,)),
            dma((3,)),
            dma((3,)),
            dma((3,)),
            dma((2, 3)),
            dma((2, 3)),
            dma((2, 2, 3)),
            dma((2, 2, 3)),
            dma,
            dma,
            dma,
            dma((2,)),
            dma((7, 3)),
            dma((7, 3)),
            dma((7, 2, 2, 3)),
            dma((7, 2, 2, 3)),
            dma((7, 7)),
            dma((7, 7)),
            dma,
            dma,
            dma,
            dma((3,)),
            dma((3,)),
            dma,
        ],
        compiler_params=pltpu.CompilerParams(collective_id=0, has_side_effects=True, vmem_limit_bytes=58 << 20),
    )(x, lengths, w_qkv, w_attn_out, w_in, w_down, ln_gain, ln_bias)


def per_device(hidden_in, lengths, w_qkv, w_attn_out, w_in, w_down, ln_gain, ln_bias):
    return layer(hidden_in, lengths, w_qkv, w_attn_out, w_in, w_down, ln_gain, ln_bias)


def solution(mesh):
    rows = P(("seq", "head"), None)
    in_specs = (P(None, "seq", None), P(), rows, rows, rows, rows, P(), P())
    out_specs = (P(None, "seq", "head"),) * 3
    return jax.shard_map(per_device, mesh=mesh, in_specs=in_specs, out_specs=out_specs, check_vma=False)
```

```python
import math

import jax
import jax.numpy as jnp
from jax import lax
from jax.experimental import pallas as pl
from jax.experimental.pallas import tpu as pltpu
from jax.sharding import PartitionSpec as P

MESH = pl.DeviceIdType.MESH
BF = jnp.bfloat16
F32 = jnp.float32
EPSILON = 1e-05
SCORE_FACTOR = 64 ** (-0.5) * math.log2(math.e)
DEAD = -1e30
IN_X, IN_Z = 384, 768
DOWN_X, DOWN_Z = 384, 384


class Place:
    def __init__(self):
        self.s = lax.axis_index("seq")
        self.h = lax.axis_index("head")
        self.z = self.s // 8
        self.xl = lax.rem(self.s // 4, 2)
        self.y = lax.rem(self.s, 4)
        self.xh = self.h // 2
        self.c = lax.rem(self.h, 2)
        self.x = self.xh * 2 + self.xl

    def peer(self, dim, d):
        x, y, z = self.x, self.y, self.z
        if dim == "x":
            x = lax.rem(x + d, 4)
        elif dim == "y":
            y = lax.rem(y + d, 4)
        else:
            z = lax.rem(z + d, 4)
        return (z * 8 + lax.rem(x, 2) * 4 + y, (x // 2) * 2 + self.c)

    def sibling(self):
        return (self.s, self.xh * 2 + 1 - self.c)


def duty(s, h):
    z, xl, y = s // 8, lax.rem(s // 4, 2), lax.rem(s, 4)
    r = lax.rem(y + z + 2 * lax.rem(h, 2), 4)
    return z * 3 + r, xl, r < 3


def remote(src, dst, send, recv, device):
    return pltpu.make_async_remote_copy(
        src_ref=src, dst_ref=dst, send_sem=send, recv_sem=recv, device_id=device, device_id_type=MESH
    )


class Ring:
    def __init__(self, me, view, dim, send, recv):
        self.me, self.view, self.dim, self.send, self.recv = me, view, dim, send, recv
        self.copies = {}

    def half(self, way, step):
        return (step + way) % 2 if step < 2 else way

    def go(self, way, step):
        behind = 3 if way == 0 else 1
        part = self.view(0 if step < 2 else behind, self.half(way, step))
        copy = remote(
            part, part, self.send(way, step), self.recv(way, step), self.me.peer(self.dim, 1 if way == 0 else 3)
        )
        copy.start()
        self.copies[way, step] = copy

    def came(self, way, step):
        behind = 3 if way == 0 else 1
        return self.view(behind if step < 2 else 2, self.half(way, step))


def greet(barrier, device):
    pl.semaphore_signal(barrier, inc=1, device_id=device, device_id_type=MESH)


def normalize(rows, gain, shift):
    average = jnp.mean(rows, axis=1, keepdims=True)
    spread = jnp.mean(rows * rows, axis=1, keepdims=True) - average * average
    return (rows - average) * lax.rsqrt(spread + EPSILON) * gain + shift


def layer_kernel(
    x_hbm, len_ref, qkv_hbm, out_hbm, in_hbm, down_hbm, gain_ref, bias_ref, hidden_hbm, kc_hbm, vc_hbm,
    x_ref, qkv_f32, out_f32, in_f32, down_f32, other, qkv_half, in_half, out_half,
    slab, w_qkv, w_in, w_out, w_down, outbox, inbox, q_aug, k_aug, v_aug, attended, joined, hidden, result,
    caches, load_sem, swap_send, swap_recv, one_send, one_recv, two_send, two_recv, three_send, three_recv,
    box_own, box_send, box_recv, cache_sem, first_send, first_recv, ring_send, ring_recv,
    share_send, share_recv, mix_send, mix_recv, mix_own, back_send, back_recv, back_own,
):
    me = Place()
    prompt, pair, busy = duty(me.s, me.h)
    sibling = me.sibling()
    loads = [
        pltpu.make_async_copy(source, target, load_sem.at[n])
        for n, (source, target) in enumerate(
            (
                (qkv_hbm, qkv_f32), (out_hbm, out_f32), (in_hbm, in_f32), (down_hbm, down_f32), (x_hbm, x_ref),
            )
        )
    ]
    for copy in loads:
        copy.start()
    barrier = pltpu.get_barrier_semaphore()

    def greet_seq(i, carry):
        greet(barrier, (lax.rem(me.s + i, 32), me.h))
        return carry

    greet(barrier, sibling)
    for xl in range(2):
        greet(barrier, (me.z * 8 + xl * 4 + me.y, (1 - me.xh) * 2 + me.c))
    lax.fori_loop(1, 32, greet_seq, 0)

    loads[0].wait()
    for k in range(2):
        for t in range(3):
            at = pl.multiple_of(t * 1024 + (2 * k + 1 - me.c) * 256, 256)
            other[:, k * 768 + t * 256 : k * 768 + (t + 1) * 256] = qkv_f32[:, pl.ds(at, 256)]
    loads[1].wait()
    loads[2].wait()
    there = 1 - me.c
    swaps = [
        remote(other, qkv_half, swap_send.at[0], swap_recv.at[0], sibling),
        remote(
            out_f32.at[:, pl.ds(pl.multiple_of(there * 512, 512), 512)],
            out_half, swap_send.at[1], swap_recv.at[1], sibling,
        ),
        remote(
            in_f32.at[:, pl.ds(pl.multiple_of(there * 2048, 2048), 2048)],
            in_half, swap_send.at[2], swap_recv.at[2], sibling,
        ),
    ]
    pl.semaphore_wait(barrier, 34)
    for copy in swaps:
        copy.start()
    loads[3].wait()
    w_down[me.z, me.xl, me.y, me.xh, me.c] = down_f32[...].astype(BF)
    first = me.c == 0

    def stack(mine, sent):
        rows = jnp.concatenate([jnp.where(first, mine, sent), jnp.where(first, sent, mine)], axis=0)
        return rows.astype(BF)

    swaps[0].wait_recv()
    for k in range(2):
        for t in range(3):
            at = pl.multiple_of(t * 1024 + (2 * k + me.c) * 256, 256)
            cols = slice(k * 768 + t * 256, k * 768 + (t + 1) * 256)
            slab[k, :, t * 256 : (t + 1) * 256] = stack(qkv_f32[:, pl.ds(at, 256)], qkv_half[:, cols])
    w_qkv[me.z, me.xl, me.y, me.xh] = slab[me.xh]
    pending = []
    one = []
    for d in (1, 3, 2):
        target = me.peer("x", d)
        copy = remote(
            slab.at[target[1] // 2], w_qkv.at[me.z, me.xl, me.y, me.xh], one_send.at[d - 1], one_recv.at[d - 1], target
        )
        copy.start()
        one.append(copy)
    pending += one

    for n, (source, half, width, target) in enumerate(
        ((out_f32, out_half, 512, w_out), (in_f32, in_half, 2048, w_in))
    ):
        swaps[n + 1].wait_recv()
        mine = source[:, pl.ds(pl.multiple_of(me.c * width, width), width)]
        target[me.c, me.z, me.xl, me.y, me.xh] = stack(mine, half[...])

    one_c = pl.ds(me.c, 1)

    def region(piece, zs, xls, ys, xhs):
        rows16, rows32 = pl.ds(0, 16), pl.ds(0, 32)
        if piece == 0:
            return w_out.at[one_c, zs, xls, ys, xhs, rows16, pl.ds(0, 512)]
        start, stop = cuts[piece]
        if piece < 4:
            return w_in.at[one_c, zs, xls, ys, xhs, rows16, pl.ds(start, stop - start)]
        return w_down.at[zs, xls, ys, xhs, one_c, rows32, pl.ds(start, stop - start)]

    cuts = {
        1: (0, IN_X), 2: (IN_X, IN_X + IN_Z), 3: (IN_X + IN_Z, 2048),
        4: (0, DOWN_X), 5: (DOWN_X, DOWN_X + DOWN_Z), 6: (DOWN_X + DOWN_Z, 1024),
    }
    order = {0: "yzx", 1: "yzx", 2: "xyz", 3: "zxy", 4: "yzx", 5: "xyz", 6: "zxy"}
    early, late = (0, 1, 2, 3), (4, 5, 6)
    pieces = early + late

    def area(piece, done, at=None, half=None):
        x, y, z = me.x, me.y, me.z
        if at is not None:
            dim, d = at
            x = lax.rem(x + d, 4) if dim == "x" else x
            y = lax.rem(y + d, 4) if dim == "y" else y
            z = lax.rem(z + d, 4) if dim == "z" else z
        zs = pl.ds(0, 4) if "z" in done else pl.ds(z, 1)
        ys = pl.ds(0, 4) if "y" in done else pl.ds(y, 1)
        xls = pl.ds(0, 2) if "x" in done else pl.ds(lax.rem(x, 2), 1)
        xhs = pl.ds(0, 2) if "x" in done else pl.ds(x // 2, 1)
        if half is not None:
            if "z" in done:
                zs = pl.ds(half * 2, 2)
            elif "y" in done:
                ys = pl.ds(half * 2, 2)
            else:
                xls = pl.ds(half, 1)
        return region(piece, zs, xls, ys, xhs)

    def send_first():
        started = []
        for piece in pieces:
            part = area(piece, "")
            for d in (1, 3, 2):
                copy = remote(
                    part, part, first_send.at[piece, d - 1], first_recv.at[piece, d - 1], me.peer(order[piece][0], d)
                )
                copy.start()
                started.append(copy)
                pending.append(copy)
        return started

    shares = {}

    def share(piece, slot, part):
        copy = remote(part, part, share_send.at[piece, slot], share_recv.at[piece, slot], sibling)
        copy.start()
        shares[piece, slot] = copy
        pending.append(copy)

    rings = {}
    for piece in pieces:
        for phase in (1, 2):
            dims = order[piece]
            rings[piece, phase] = Ring(
                me,
                lambda d, half, piece=piece, dims=dims, phase=phase: area(piece, dims[:phase], (dims[phase], d), half),
                dims[phase],
                lambda way, step, piece=piece, phase=phase: ring_send.at[piece, phase - 1, way, step],
                lambda way, step, piece=piece, phase=phase: ring_recv.at[piece, phase - 1, way, step],
            )

    def start(which, step):
        for ring in which:
            for way in range(2):
                ring.go(way, step)

    def take(which, step):
        for ring in which:
            for way in range(2):
                ring.copies[way, step].wait_recv()
                if step == 0:
                    ring.go(way, 2)

    def ring_start(group, step):
        start([rings[piece, 2] for piece in group], step)

    def ring_take(group, step):
        for piece in group:
            ring = rings[piece, 2]
            take([ring], step)
            for way in range(2):
                share(piece, 1 + way * 3 + step, ring.came(way, step))

    bulk_one = send_first()
    for copy in one:
        copy.wait_recv()
    left, right = pl.ds(0, 384), pl.ds(384, 384)
    all2, all4, all16 = pl.ds(0, 2), pl.ds(0, 4), pl.ds(0, 16)
    zs, ys = pl.ds(me.z, 1), pl.ds(me.y, 1)
    two = []
    for d in (1, 3, 2):
        for k, (dim, cols) in enumerate((("y", left), ("z", right))):
            part = w_qkv.at[zs, all2, ys, all2, all16, cols]
            copy = remote(part, part, two_send.at[k, d - 1], two_recv.at[k, d - 1], me.peer(dim, d))
            copy.start()
            two.append(copy)
    pending += two
    for copy in bulk_one:
        copy.wait_recv()
    middle = [rings[piece, 1] for piece in pieces]
    start(middle, 0)
    start(middle, 1)
    for copy in two:
        copy.wait_recv()

    def view_left(d, half):
        return w_qkv.at[pl.ds(lax.rem(me.z + d, 4), 1), all2, pl.ds(half * 2, 2), all2, all16, left]

    def view_right(d, half):
        return w_qkv.at[pl.ds(half * 2, 2), all2, pl.ds(lax.rem(me.y + d, 4), 1), all2, all16, right]

    three = [
        Ring(
            me, view, dim,
            lambda way, step, k=k: three_send.at[k, way, step],
            lambda way, step, k=k: three_recv.at[k, way, step],
        )
        for k, (view, dim) in enumerate(((view_left, "z"), (view_right, "y")))
    ]
    start(three, 0)
    start(three, 1)
    take(three, 0)
    take(middle, 0)
    loads[4].wait()
    take(three, 1)
    take(three, 2)

    for t in range(3):
        w = w_qkv[:, :, :, :, :, t * 256 : (t + 1) * 256].reshape(1024, 256)
        for g in range(2):
            rows = x_ref[g * 6 : (g + 1) * 6].reshape(384, 1024)
            got = jnp.dot(rows, w, preferred_element_type=F32)
            for q in range(6):
                p = g * 6 + q
                piece = got[q * 64 : (q + 1) * 64]
                if t > 0:
                    at = me.s * 64 + lax.broadcasted_iota(jnp.int32, (64, 256), 0)
                    piece = jnp.where(at < len_ref[p], piece, 0.0)
                piece = piece.astype(BF)
                if t > 0:
                    caches[t - 1, p] = piece
                outbox[p * 2, t] = piece[:, :128]
                outbox[p * 2 + 1, t] = piece[:, 128:]

    def post(i, carry):
        to = lax.rem(me.s + i, 32)
        their_prompt, their_pair, their_busy = duty(to, me.h)

        @pl.when(their_busy)
        def _():
            remote(
                outbox.at[their_prompt * 2 + their_pair], inbox.at[:, me.s], box_send, box_recv, (to, me.h)
            ).start()

        return carry

    lax.fori_loop(1, 32, post, 0)
    keeps = [
        pltpu.make_async_copy(caches.at[0], kc_hbm, cache_sem.at[0]),
        pltpu.make_async_copy(caches.at[1], vc_hbm, cache_sem.at[1]),
    ]
    for copy in keeps:
        copy.start()

    take(middle, 1)
    take(middle, 2)
    ring_start(early, 0)
    ring_start(early, 1)
    for piece in pieces:
        share(piece, 0, area(piece, order[piece][:2]))
    ring_take(early, 0)
    ring_start(late, 0)
    ring_take(early, 1)
    ring_start(late, 1)

    @pl.when(busy)
    def _():
        keep = pltpu.make_async_copy(outbox.at[prompt * 2 + pair], inbox.at[:, me.s], box_own)
        keep.start()
        keep.wait()
        arrived = inbox.at[:, pl.ds(0, 31)]
        pltpu.make_async_copy(arrived, arrived, box_recv).wait()
        lane = lax.broadcasted_iota(jnp.int32, (2048, 128), 1)
        place = lax.broadcasted_iota(jnp.int32, (2048, 128), 0)
        bias = jnp.where(place < len_ref[prompt], 0.0, DEAD)
        q = inbox[0].reshape(2048, 128).astype(F32)
        k = inbox[1].reshape(2048, 128).astype(F32)
        v = inbox[2].reshape(2048, 128).astype(F32)
        for n in range(2):
            own = (lane // 64) == n
            mark = lane == (1 - n) * 64
            q_aug[n] = jnp.where(own, q, jnp.where(mark, 1.0, 0.0)).astype(BF)
            k_aug[n] = jnp.where(mark, bias, k).astype(BF)
            v_aug[n] = jnp.where(own, v, 1.0).astype(BF)

    low = lax.broadcasted_iota(jnp.int32, (256, 128), 1) < 64
    columns = pl.ds(pl.multiple_of((me.h * 2 + pair) * 128, 128), 128)
    slot = lax.rem(prompt, 3)
    lands_here = me.h == me.z

    def attend(start, stop):
        @pl.when(busy)
        def _():
            def block(i, carry):
                rows = pl.ds(pl.multiple_of(i * 256, 256), 256)
                mixed = []
                for n in range(2):
                    scores = lax.dot_general(
                        q_aug[n, rows, :], k_aug[n], (((1,), (1,)), ((), ())), preferred_element_type=F32
                    )
                    top = jnp.max(scores, axis=1, keepdims=True)
                    terms = jnp.exp2((scores - top) * SCORE_FACTOR).astype(BF)
                    got = jnp.dot(terms, v_aug[n], preferred_element_type=F32)
                    mixed.append(got / pltpu.roll(got, 64, 1))
                both = jnp.where(low, mixed[0], mixed[1]).astype(BF)
                attended[pl.ds(i * 4, 4)] = both.reshape(4, 64, 128)
                for k in range(4):
                    to = i * 4 + k
                    stays = jnp.logical_and(lands_here, to == me.s)

                    @pl.when(stays)
                    def _():
                        pltpu.make_async_copy(attended.at[to], joined.at[slot, :, columns], mix_own).start()

                    @pl.when(jnp.logical_not(stays))
                    def _():
                        remote(
                            attended.at[to], joined.at[slot, :, columns], mix_send, mix_recv, (to, me.z)
                        ).start()

                return carry

            lax.fori_loop(start, stop, block, 0)

    attend(0, 2)
    ring_take(early, 2)
    attend(2, 6)
    ring_take(late, 0)
    attend(6, 8)
    ring_take(late, 1)
    mine_too = jnp.logical_and(busy, lands_here)

    @pl.when(mine_too)
    def _():
        pltpu.make_async_copy(attended.at[me.s], joined.at[slot, :, columns], mix_own).wait()
        part = attended.at[pl.ds(0, 23)]
        pltpu.make_async_copy(part, part, mix_recv).wait()

    @pl.when(jnp.logical_not(mine_too))
    def _():
        part = attended.at[pl.ds(0, 24)]
        pltpu.make_async_copy(part, part, mix_recv).wait()

    for key, copy in shares.items():
        if key[0] in early:
            copy.wait_recv()

    x_rows = x_ref[pl.ds(me.h * 3, 3)].reshape(192, 1024).astype(F32)
    mixed = joined[...].reshape(192, 1024)
    sums = jnp.concatenate(
        [jnp.dot(mixed, w_out[n].reshape(1024, 512), preferred_element_type=F32) for n in range(2)], axis=1
    )
    normed = normalize(sums + x_rows, gain_ref[0:1], bias_ref[0:1]).astype(BF)
    for n in range(2):
        for k in range(4):
            w = w_in[n, :, :, :, :, :, k * 512 : (k + 1) * 512].reshape(1024, 512)
            units = jnp.dot(normed, w, preferred_element_type=F32)
            units = 0.5 * units * (1.0 + lax.erf(units * (2.0**-0.5)))
            hidden[n * 4 + k] = units.astype(BF)
    ring_take(late, 2)
    for key, copy in shares.items():
        if key[0] in late:
            copy.wait_recv()
    total = normed.astype(F32)
    for k in range(8):
        w = w_down[k // 2, k % 2].reshape(512, 1024)
        total = total + jnp.dot(hidden[k], w, preferred_element_type=F32)
    final = normalize(total, gain_ref[1:2], bias_ref[1:2]).astype(BF)
    for n in range(4):
        result[n] = final[:, n * 256 : (n + 1) * 256].reshape(3, 64, 256)
    rows = pl.ds(me.h * 3, 3)
    own = pltpu.make_async_copy(result.at[me.h], hidden_hbm.at[rows], back_own)
    own.start()
    last = []
    for d in range(1, 4):
        to = lax.rem(me.h + d, 4)
        copy = remote(result.at[to], hidden_hbm.at[rows], back_send.at[d - 1], back_recv.at[d - 1], (me.s, to))
        copy.start()
        last.append(copy)

    @pl.when(busy)
    def _():
        gone = outbox.at[pl.ds(0, 23)]
        pltpu.make_async_copy(gone, gone, box_send).wait()

    @pl.when(jnp.logical_not(busy))
    def _():
        gone = outbox.at[pl.ds(0, 24)]
        pltpu.make_async_copy(gone, gone, box_send).wait()

    @pl.when(mine_too)
    def _():
        part = attended.at[pl.ds(0, 31)]
        pltpu.make_async_copy(part, part, mix_send).wait()

    @pl.when(jnp.logical_and(busy, jnp.logical_not(lands_here)))
    def _():
        pltpu.make_async_copy(attended, attended, mix_send).wait()

    for ring in [*rings.values(), *three]:
        pending += ring.copies.values()
    for copy in swaps + pending:
        copy.wait_send()
    for copy in keeps:
        copy.wait()
    own.wait()
    for copy in last:
        copy.wait()


def layer(x, lengths, w_qkv, w_attn_out, w_in, w_down, ln_gain, ln_bias):
    vmem, free = pl.BlockSpec(memory_space=pltpu.VMEM), pl.BlockSpec(memory_space=pl.ANY)
    hbm = pl.BlockSpec(memory_space=pltpu.HBM)
    dma = pltpu.SemaphoreType.DMA
    return pl.pallas_call(
        layer_kernel,
        out_shape=(jax.ShapeDtypeStruct((12, 64, 256), BF),) * 3,
        in_specs=[hbm, pl.BlockSpec(memory_space=pltpu.SMEM), hbm, hbm, hbm, hbm, vmem, vmem],
        out_specs=(free,) * 3,
        scratch_shapes=[
            pltpu.VMEM((12, 64, 1024), BF),
            pltpu.VMEM((8, 3072), F32),
            pltpu.VMEM((8, 1024), F32),
            pltpu.VMEM((8, 4096), F32),
            pltpu.VMEM((32, 1024), F32),
            pltpu.VMEM((8, 1536), F32),
            pltpu.VMEM((8, 1536), F32),
            pltpu.VMEM((8, 2048), F32),
            pltpu.VMEM((8, 512), F32),
            pltpu.VMEM((2, 16, 768), BF),
            pltpu.VMEM((4, 2, 4, 2, 16, 768), BF),
            pltpu.VMEM((2, 4, 2, 4, 2, 16, 2048), BF),
            pltpu.VMEM((2, 4, 2, 4, 2, 16, 512), BF),
            pltpu.VMEM((4, 2, 4, 2, 2, 32, 1024), BF),
            pltpu.VMEM((24, 3, 64, 128), BF),
            pltpu.VMEM((3, 32, 64, 128), BF),
            pltpu.VMEM((2, 2048, 128), BF),
            pltpu.VMEM((2, 2048, 128), BF),
            pltpu.VMEM((2, 2048, 128), BF),
            pltpu.VMEM((32, 64, 128), BF),
            pltpu.VMEM((3, 64, 1024), BF),
            pltpu.VMEM((8, 192, 512), BF),
            pltpu.VMEM((4, 3, 64, 256), BF),
            pltpu.VMEM((2, 12, 64, 256), BF),
            dma((5,)),
            dma((3,)),
            dma((3,)),
            dma((3,)),
            dma((3,)),
            dma((2, 3)),
            dma((2, 3)),
            dma((2, 2, 3)),
            dma((2, 2, 3)),
            dma,
            dma,
            dma,
            dma((2,)),
            dma((7, 3)),
            dma((7, 3)),
            dma((7, 2, 2, 3)),
            dma((7, 2, 2, 3)),
            dma((7, 7)),
            dma((7, 7)),
            dma,
            dma,
            dma,
            dma((3,)),
            dma((3,)),
            dma,
        ],
        compiler_params=pltpu.CompilerParams(collective_id=0, has_side_effects=True, vmem_limit_bytes=46 << 20),
    )(x, lengths, w_qkv, w_attn_out, w_in, w_down, ln_gain, ln_bias)


def hand_over(*refs):
    copies = [pltpu.make_async_copy(refs[n], refs[3 + n], refs[6].at[n]) for n in range(3)]
    for copy in copies:
        copy.start()
    for copy in copies:
        copy.wait()


def per_device(hidden_in, lengths, w_qkv, w_attn_out, w_in, w_down, ln_gain, ln_bias):
    operands = (hidden_in, lengths, w_qkv, w_attn_out, w_in, w_down, ln_gain, ln_bias)
    made = layer(*(pltpu.with_memory_space_constraint(a, pltpu.HBM) for a in operands))
    return pl.pallas_call(
        hand_over,
        out_shape=tuple(jax.ShapeDtypeStruct(part.shape, part.dtype) for part in made),
        in_specs=[pl.BlockSpec(memory_space=pl.ANY)] * 3,
        out_specs=(pl.BlockSpec(memory_space=pltpu.HBM),) * 3,
        scratch_shapes=[pltpu.SemaphoreType.DMA((3,))],
        compiler_params=pltpu.CompilerParams(vmem_limit_bytes=1 << 20),
    )(*made)


def solution(mesh):
    rows = P(("seq", "head"), None)
    in_specs = (P(None, "seq", None), P(), rows, rows, rows, rows, P(), P())
    out_specs = (P(None, "seq", "head"),) * 3
    return jax.shard_map(per_device, mesh=mesh, in_specs=in_specs, out_specs=out_specs, check_vma=False)
```

```python
import math

import jax
import jax.numpy as jnp
from jax import lax
from jax.experimental import pallas as pl
from jax.experimental.pallas import tpu as pltpu
from jax.sharding import PartitionSpec as P

MESH = pl.DeviceIdType.MESH
BF = jnp.bfloat16
F32 = jnp.float32
EPSILON = 1e-05
SCORE_FACTOR = 64 ** (-0.5) * math.log2(math.e)
DEAD = -1e30
IN_X, IN_Z = 384, 768
DOWN_X, DOWN_Z = 384, 384


class Place:
    def __init__(self):
        self.s = lax.axis_index("seq")
        self.h = lax.axis_index("head")
        self.z = self.s // 8
        self.xl = lax.rem(self.s // 4, 2)
        self.y = lax.rem(self.s, 4)
        self.xh = self.h // 2
        self.c = lax.rem(self.h, 2)
        self.x = self.xh * 2 + self.xl

    def peer(self, dim, d):
        x, y, z = self.x, self.y, self.z
        if dim == "x":
            x = lax.rem(x + d, 4)
        elif dim == "y":
            y = lax.rem(y + d, 4)
        else:
            z = lax.rem(z + d, 4)
        return (z * 8 + lax.rem(x, 2) * 4 + y, (x // 2) * 2 + self.c)

    def sibling(self):
        return (self.s, self.xh * 2 + 1 - self.c)


def duty(s, h):
    z, xl, y = s // 8, lax.rem(s // 4, 2), lax.rem(s, 4)
    r = lax.rem(y + z + 2 * lax.rem(h, 2), 4)
    return z * 3 + r, xl, r < 3


def remote(src, dst, send, recv, device):
    return pltpu.make_async_remote_copy(
        src_ref=src, dst_ref=dst, send_sem=send, recv_sem=recv, device_id=device, device_id_type=MESH
    )


class Ring:
    def __init__(self, me, view, dim, send, recv):
        self.me, self.view, self.dim, self.send, self.recv = me, view, dim, send, recv
        self.copies = {}

    def half(self, way, step):
        return (step + way) % 2 if step < 2 else way

    def go(self, way, step):
        behind = 3 if way == 0 else 1
        part = self.view(0 if step < 2 else behind, self.half(way, step))
        copy = remote(
            part, part, self.send(way, step), self.recv(way, step), self.me.peer(self.dim, 1 if way == 0 else 3)
        )
        copy.start()
        self.copies[way, step] = copy

    def came(self, way, step):
        behind = 3 if way == 0 else 1
        return self.view(behind if step < 2 else 2, self.half(way, step))


def greet(barrier, device):
    pl.semaphore_signal(barrier, inc=1, device_id=device, device_id_type=MESH)


def normalize(rows, gain, shift):
    average = jnp.mean(rows, axis=1, keepdims=True)
    spread = jnp.mean(rows * rows, axis=1, keepdims=True) - average * average
    return (rows - average) * lax.rsqrt(spread + EPSILON) * gain + shift


def layer_kernel(
    x_hbm, len_ref, qkv_hbm, out_hbm, in_hbm, down_hbm, gain_ref, bias_ref, hidden_hbm, kc_hbm, vc_hbm,
    x_ref, qkv_f32, out_f32, in_f32, down_f32, other, qkv_half, in_half, out_half,
    slab, w_qkv, w_in, w_out, w_down, outbox, inbox, q_aug, k_aug, v_aug, attended, joined, hidden, result,
    caches, load_sem, swap_send, swap_recv, one_send, one_recv, two_send, two_recv, three_send, three_recv,
    box_own, box_send, box_recv, cache_sem, first_send, first_recv, ring_send, ring_recv,
    share_send, share_recv, mix_send, mix_recv, mix_own, back_send, back_recv, back_own,
):
    me = Place()
    prompt, pair, busy = duty(me.s, me.h)
    sibling = me.sibling()
    loads = [
        pltpu.make_async_copy(source, target, load_sem.at[n])
        for n, (source, target) in enumerate(
            (
                (qkv_hbm, qkv_f32), (out_hbm, out_f32), (in_hbm, in_f32), (down_hbm, down_f32), (x_hbm, x_ref),
            )
        )
    ]
    for copy in loads:
        copy.start()
    barrier = pltpu.get_barrier_semaphore()

    def greet_seq(i, carry):
        greet(barrier, (lax.rem(me.s + i, 32), me.h))
        return carry

    greet(barrier, sibling)
    for xl in range(2):
        greet(barrier, (me.z * 8 + xl * 4 + me.y, (1 - me.xh) * 2 + me.c))
    lax.fori_loop(1, 32, greet_seq, 0)

    loads[0].wait()
    for k in range(2):
        for t in range(3):
            at = pl.multiple_of(t * 1024 + (2 * k + 1 - me.c) * 256, 256)
            other[:, k * 768 + t * 256 : k * 768 + (t + 1) * 256] = qkv_f32[:, pl.ds(at, 256)]
    loads[1].wait()
    loads[2].wait()
    there = 1 - me.c
    swaps = [
        remote(other, qkv_half, swap_send.at[0], swap_recv.at[0], sibling),
        remote(
            out_f32.at[:, pl.ds(pl.multiple_of(there * 512, 512), 512)],
            out_half, swap_send.at[1], swap_recv.at[1], sibling,
        ),
        remote(
            in_f32.at[:, pl.ds(pl.multiple_of(there * 2048, 2048), 2048)],
            in_half, swap_send.at[2], swap_recv.at[2], sibling,
        ),
    ]
    loads[3].wait()
    w_down[me.z, me.xl, me.y, me.xh, me.c] = down_f32[...].astype(BF)
    pl.semaphore_wait(barrier, 34)
    for copy in swaps:
        copy.start()
    first = me.c == 0

    def stack(mine, sent):
        rows = jnp.concatenate([jnp.where(first, mine, sent), jnp.where(first, sent, mine)], axis=0)
        return rows.astype(BF)

    pending = []
    one_c = pl.ds(me.c, 1)

    def region(piece, zs, xls, ys, xhs):
        rows16, rows32 = pl.ds(0, 16), pl.ds(0, 32)
        if piece == 0:
            return w_out.at[one_c, zs, xls, ys, xhs, rows16, pl.ds(0, 512)]
        start, stop = cuts[piece]
        if piece < 4:
            return w_in.at[one_c, zs, xls, ys, xhs, rows16, pl.ds(start, stop - start)]
        return w_down.at[zs, xls, ys, xhs, one_c, rows32, pl.ds(start, stop - start)]

    cuts = {
        1: (0, IN_X), 2: (IN_X, IN_X + IN_Z), 3: (IN_X + IN_Z, 2048),
        4: (0, DOWN_X), 5: (DOWN_X, DOWN_X + DOWN_Z), 6: (DOWN_X + DOWN_Z, 1024),
    }
    order = {0: "yzx", 1: "yzx", 2: "xyz", 3: "zxy", 4: "yzx", 5: "xyz", 6: "zxy"}
    early, late = (0, 1, 2, 3), (4, 5, 6)
    pieces = early + late

    def area(piece, done, at=None, half=None):
        x, y, z = me.x, me.y, me.z
        if at is not None:
            dim, d = at
            x = lax.rem(x + d, 4) if dim == "x" else x
            y = lax.rem(y + d, 4) if dim == "y" else y
            z = lax.rem(z + d, 4) if dim == "z" else z
        zs = pl.ds(0, 4) if "z" in done else pl.ds(z, 1)
        ys = pl.ds(0, 4) if "y" in done else pl.ds(y, 1)
        xls = pl.ds(0, 2) if "x" in done else pl.ds(lax.rem(x, 2), 1)
        xhs = pl.ds(0, 2) if "x" in done else pl.ds(x // 2, 1)
        if half is not None:
            if "z" in done:
                zs = pl.ds(half * 2, 2)
            elif "y" in done:
                ys = pl.ds(half * 2, 2)
            else:
                xls = pl.ds(half, 1)
        return region(piece, zs, xls, ys, xhs)

    def send_first(group):
        started = []
        for piece in group:
            part = area(piece, "")
            for d in (1, 3, 2):
                copy = remote(
                    part, part, first_send.at[piece, d - 1], first_recv.at[piece, d - 1], me.peer(order[piece][0], d)
                )
                copy.start()
                started.append(copy)
                pending.append(copy)
        return started

    late_one = send_first(late)
    swaps[0].wait_recv()
    for k in range(2):
        for t in range(3):
            at = pl.multiple_of(t * 1024 + (2 * k + me.c) * 256, 256)
            cols = slice(k * 768 + t * 256, k * 768 + (t + 1) * 256)
            slab[k, :, t * 256 : (t + 1) * 256] = stack(qkv_f32[:, pl.ds(at, 256)], qkv_half[:, cols])
    w_qkv[me.z, me.xl, me.y, me.xh] = slab[me.xh]
    one = []
    for d in (1, 3, 2):
        target = me.peer("x", d)
        copy = remote(
            slab.at[target[1] // 2], w_qkv.at[me.z, me.xl, me.y, me.xh], one_send.at[d - 1], one_recv.at[d - 1], target
        )
        copy.start()
        one.append(copy)
    pending += one

    for n, (source, half, width, target) in enumerate(
        ((out_f32, out_half, 512, w_out), (in_f32, in_half, 2048, w_in))
    ):
        swaps[n + 1].wait_recv()
        mine = source[:, pl.ds(pl.multiple_of(me.c * width, width), width)]
        target[me.c, me.z, me.xl, me.y, me.xh] = stack(mine, half[...])

    shares = {}

    def share(piece, slot, part):
        copy = remote(part, part, share_send.at[piece, slot], share_recv.at[piece, slot], sibling)
        copy.start()
        shares[piece, slot] = copy
        pending.append(copy)

    rings = {}
    for piece in pieces:
        for phase in (1, 2):
            dims = order[piece]
            rings[piece, phase] = Ring(
                me,
                lambda d, half, piece=piece, dims=dims, phase=phase: area(piece, dims[:phase], (dims[phase], d), half),
                dims[phase],
                lambda way, step, piece=piece, phase=phase: ring_send.at[piece, phase - 1, way, step],
                lambda way, step, piece=piece, phase=phase: ring_recv.at[piece, phase - 1, way, step],
            )

    def start(which, step):
        for ring in which:
            for way in range(2):
                ring.go(way, step)

    def take(which, step):
        for ring in which:
            for way in range(2):
                ring.copies[way, step].wait_recv()
                if step == 0:
                    ring.go(way, 2)

    def ring_start(group, step):
        start([rings[piece, 2] for piece in group], step)

    def ring_take(group, step):
        for piece in group:
            ring = rings[piece, 2]
            take([ring], step)
            for way in range(2):
                share(piece, 1 + way * 3 + step, ring.came(way, step))

    bulk_one = send_first(early)
    middle = [rings[piece, 1] for piece in late]
    for copy in late_one:
        copy.wait_recv()
    start(middle, 0)
    start(middle, 1)
    for copy in one:
        copy.wait_recv()
    left, right = pl.ds(0, 384), pl.ds(384, 384)
    all2, all4, all16 = pl.ds(0, 2), pl.ds(0, 4), pl.ds(0, 16)
    zs, ys = pl.ds(me.z, 1), pl.ds(me.y, 1)
    two = []
    for d in (1, 3, 2):
        for k, (dim, cols) in enumerate((("y", left), ("z", right))):
            part = w_qkv.at[zs, all2, ys, all2, all16, cols]
            copy = remote(part, part, two_send.at[k, d - 1], two_recv.at[k, d - 1], me.peer(dim, d))
            copy.start()
            two.append(copy)
    pending += two
    for copy in bulk_one:
        copy.wait_recv()
    middle = [rings[piece, 1] for piece in early]
    start(middle, 0)
    start(middle, 1)
    middle = [rings[piece, 1] for piece in pieces]
    for copy in two:
        copy.wait_recv()

    def view_left(d, half):
        return w_qkv.at[pl.ds(lax.rem(me.z + d, 4), 1), all2, pl.ds(half * 2, 2), all2, all16, left]

    def view_right(d, half):
        return w_qkv.at[pl.ds(half * 2, 2), all2, pl.ds(lax.rem(me.y + d, 4), 1), all2, all16, right]

    three = [
        Ring(
            me, view, dim,
            lambda way, step, k=k: three_send.at[k, way, step],
            lambda way, step, k=k: three_recv.at[k, way, step],
        )
        for k, (view, dim) in enumerate(((view_left, "z"), (view_right, "y")))
    ]
    start(three, 0)
    start(three, 1)
    take(three, 0)
    take(middle, 0)
    loads[4].wait()
    take(three, 1)
    take(three, 2)

    for t in range(3):
        w = w_qkv[:, :, :, :, :, t * 256 : (t + 1) * 256].reshape(1024, 256)
        for g in range(2):
            rows = x_ref[g * 6 : (g + 1) * 6].reshape(384, 1024)
            got = jnp.dot(rows, w, preferred_element_type=F32)
            for q in range(6):
                p = g * 6 + q
                piece = got[q * 64 : (q + 1) * 64]
                if t > 0:
                    at = me.s * 64 + lax.broadcasted_iota(jnp.int32, (64, 256), 0)
                    piece = jnp.where(at < len_ref[p], piece, 0.0)
                piece = piece.astype(BF)
                if t > 0:
                    caches[t - 1, p] = piece
                outbox[p * 2, t] = piece[:, :128]
                outbox[p * 2 + 1, t] = piece[:, 128:]

    def post(i, carry):
        to = lax.rem(me.s + i, 32)
        their_prompt, their_pair, their_busy = duty(to, me.h)

        @pl.when(their_busy)
        def _():
            remote(
                outbox.at[their_prompt * 2 + their_pair], inbox.at[:, me.s], box_send, box_recv, (to, me.h)
            ).start()

        return carry

    lax.fori_loop(1, 32, post, 0)
    keeps = [
        pltpu.make_async_copy(caches.at[0], kc_hbm, cache_sem.at[0]),
        pltpu.make_async_copy(caches.at[1], vc_hbm, cache_sem.at[1]),
    ]
    for copy in keeps:
        copy.start()

    take(middle, 1)
    take(middle, 2)
    ring_start(early, 0)
    ring_start(early, 1)
    for piece in pieces:
        share(piece, 0, area(piece, order[piece][:2]))
    ring_take(early, 0)
    ring_start(late, 0)
    ring_take(early, 1)
    ring_start(late, 1)

    @pl.when(busy)
    def _():
        keep = pltpu.make_async_copy(outbox.at[prompt * 2 + pair], inbox.at[:, me.s], box_own)
        keep.start()
        keep.wait()
        arrived = inbox.at[:, pl.ds(0, 31)]
        pltpu.make_async_copy(arrived, arrived, box_recv).wait()
        lane = lax.broadcasted_iota(jnp.int32, (2048, 128), 1)
        place = lax.broadcasted_iota(jnp.int32, (2048, 128), 0)
        bias = jnp.where(place < len_ref[prompt], 0.0, DEAD)
        q = inbox[0].reshape(2048, 128).astype(F32)
        k = inbox[1].reshape(2048, 128).astype(F32)
        v = inbox[2].reshape(2048, 128).astype(F32)
        for n in range(2):
            own = (lane // 64) == n
            mark = lane == (1 - n) * 64
            q_aug[n] = jnp.where(own, q, jnp.where(mark, 1.0, 0.0)).astype(BF)
            k_aug[n] = jnp.where(mark, bias, k).astype(BF)
            v_aug[n] = jnp.where(own, v, 1.0).astype(BF)

    low = lax.broadcasted_iota(jnp.int32, (256, 128), 1) < 64
    columns = pl.ds(pl.multiple_of((me.h * 2 + pair) * 128, 128), 128)
    slot = lax.rem(prompt, 3)
    lands_here = me.h == me.z

    def attend(start, stop):
        @pl.when(busy)
        def _():
            def block(i, carry):
                rows = pl.ds(pl.multiple_of(i * 256, 256), 256)
                mixed = []
                for n in range(2):
                    scores = lax.dot_general(
                        q_aug[n, rows, :], k_aug[n], (((1,), (1,)), ((), ())), preferred_element_type=F32
                    )
                    top = jnp.max(scores, axis=1, keepdims=True)
                    terms = jnp.exp2((scores - top) * SCORE_FACTOR).astype(BF)
                    got = jnp.dot(terms, v_aug[n], preferred_element_type=F32)
                    mixed.append(got / pltpu.roll(got, 64, 1))
                both = jnp.where(low, mixed[0], mixed[1]).astype(BF)
                attended[pl.ds(i * 4, 4)] = both.reshape(4, 64, 128)
                for k in range(4):
                    to = i * 4 + k
                    stays = jnp.logical_and(lands_here, to == me.s)

                    @pl.when(stays)
                    def _():
                        pltpu.make_async_copy(attended.at[to], joined.at[slot, :, columns], mix_own).start()

                    @pl.when(jnp.logical_not(stays))
                    def _():
                        remote(
                            attended.at[to], joined.at[slot, :, columns], mix_send, mix_recv, (to, me.z)
                        ).start()

                return carry

            lax.fori_loop(start, stop, block, 0)

    attend(0, 2)
    ring_take(early, 2)
    attend(2, 6)
    ring_take(late, 0)
    attend(6, 8)
    ring_take(late, 1)
    mine_too = jnp.logical_and(busy, lands_here)

    @pl.when(mine_too)
    def _():
        pltpu.make_async_copy(attended.at[me.s], joined.at[slot, :, columns], mix_own).wait()
        part = attended.at[pl.ds(0, 23)]
        pltpu.make_async_copy(part, part, mix_recv).wait()

    @pl.when(jnp.logical_not(mine_too))
    def _():
        part = attended.at[pl.ds(0, 24)]
        pltpu.make_async_copy(part, part, mix_recv).wait()

    for key, copy in shares.items():
        if key[0] in early:
            copy.wait_recv()

    x_rows = x_ref[pl.ds(me.h * 3, 3)].reshape(192, 1024).astype(F32)
    mixed = joined[...].reshape(192, 1024)
    sums = jnp.concatenate(
        [jnp.dot(mixed, w_out[n].reshape(1024, 512), preferred_element_type=F32) for n in range(2)], axis=1
    )
    normed = normalize(sums + x_rows, gain_ref[0:1], bias_ref[0:1]).astype(BF)
    for n in range(2):
        for k in range(4):
            w = w_in[n, :, :, :, :, :, k * 512 : (k + 1) * 512].reshape(1024, 512)
            units = jnp.dot(normed, w, preferred_element_type=F32)
            units = 0.5 * units * (1.0 + lax.erf(units * (2.0**-0.5)))
            hidden[n * 4 + k] = units.astype(BF)
    ring_take(late, 2)
    for key, copy in shares.items():
        if key[0] in late:
            copy.wait_recv()
    total = normed.astype(F32)
    for k in range(8):
        w = w_down[k // 2, k % 2].reshape(512, 1024)
        total = total + jnp.dot(hidden[k], w, preferred_element_type=F32)
    final = normalize(total, gain_ref[1:2], bias_ref[1:2]).astype(BF)
    for n in range(4):
        result[n] = final[:, n * 256 : (n + 1) * 256].reshape(3, 64, 256)
    rows = pl.ds(me.h * 3, 3)
    own = pltpu.make_async_copy(result.at[me.h], hidden_hbm.at[rows], back_own)
    own.start()
    last = []
    for d in range(1, 4):
        to = lax.rem(me.h + d, 4)
        copy = remote(result.at[to], hidden_hbm.at[rows], back_send.at[d - 1], back_recv.at[d - 1], (me.s, to))
        copy.start()
        last.append(copy)

    @pl.when(busy)
    def _():
        gone = outbox.at[pl.ds(0, 23)]
        pltpu.make_async_copy(gone, gone, box_send).wait()

    @pl.when(jnp.logical_not(busy))
    def _():
        gone = outbox.at[pl.ds(0, 24)]
        pltpu.make_async_copy(gone, gone, box_send).wait()

    @pl.when(mine_too)
    def _():
        part = attended.at[pl.ds(0, 31)]
        pltpu.make_async_copy(part, part, mix_send).wait()

    @pl.when(jnp.logical_and(busy, jnp.logical_not(lands_here)))
    def _():
        pltpu.make_async_copy(attended, attended, mix_send).wait()

    for ring in [*rings.values(), *three]:
        pending += ring.copies.values()
    for copy in swaps + pending:
        copy.wait_send()
    for copy in keeps:
        copy.wait()
    own.wait()
    for copy in last:
        copy.wait()


def layer(x, lengths, w_qkv, w_attn_out, w_in, w_down, ln_gain, ln_bias):
    vmem, free = pl.BlockSpec(memory_space=pltpu.VMEM), pl.BlockSpec(memory_space=pl.ANY)
    hbm = pl.BlockSpec(memory_space=pltpu.HBM)
    dma = pltpu.SemaphoreType.DMA
    return pl.pallas_call(
        layer_kernel,
        out_shape=(jax.ShapeDtypeStruct((12, 64, 256), BF),) * 3,
        in_specs=[hbm, pl.BlockSpec(memory_space=pltpu.SMEM), hbm, hbm, hbm, hbm, vmem, vmem],
        out_specs=(free,) * 3,
        scratch_shapes=[
            pltpu.VMEM((12, 64, 1024), BF),
            pltpu.VMEM((8, 3072), F32),
            pltpu.VMEM((8, 1024), F32),
            pltpu.VMEM((8, 4096), F32),
            pltpu.VMEM((32, 1024), F32),
            pltpu.VMEM((8, 1536), F32),
            pltpu.VMEM((8, 1536), F32),
            pltpu.VMEM((8, 2048), F32),
            pltpu.VMEM((8, 512), F32),
            pltpu.VMEM((2, 16, 768), BF),
            pltpu.VMEM((4, 2, 4, 2, 16, 768), BF),
            pltpu.VMEM((2, 4, 2, 4, 2, 16, 2048), BF),
            pltpu.VMEM((2, 4, 2, 4, 2, 16, 512), BF),
            pltpu.VMEM((4, 2, 4, 2, 2, 32, 1024), BF),
            pltpu.VMEM((24, 3, 64, 128), BF),
            pltpu.VMEM((3, 32, 64, 128), BF),
            pltpu.VMEM((2, 2048, 128), BF),
            pltpu.VMEM((2, 2048, 128), BF),
            pltpu.VMEM((2, 2048, 128), BF),
            pltpu.VMEM((32, 64, 128), BF),
            pltpu.VMEM((3, 64, 1024), BF),
            pltpu.VMEM((8, 192, 512), BF),
            pltpu.VMEM((4, 3, 64, 256), BF),
            pltpu.VMEM((2, 12, 64, 256), BF),
            dma((5,)),
            dma((3,)),
            dma((3,)),
            dma((3,)),
            dma((3,)),
            dma((2, 3)),
            dma((2, 3)),
            dma((2, 2, 3)),
            dma((2, 2, 3)),
            dma,
            dma,
            dma,
            dma((2,)),
            dma((7, 3)),
            dma((7, 3)),
            dma((7, 2, 2, 3)),
            dma((7, 2, 2, 3)),
            dma((7, 7)),
            dma((7, 7)),
            dma,
            dma,
            dma,
            dma((3,)),
            dma((3,)),
            dma,
        ],
        compiler_params=pltpu.CompilerParams(collective_id=0, has_side_effects=True, vmem_limit_bytes=46 << 20),
    )(x, lengths, w_qkv, w_attn_out, w_in, w_down, ln_gain, ln_bias)


def hand_over(*refs):
    copies = [pltpu.make_async_copy(refs[n], refs[3 + n], refs[6].at[n]) for n in range(3)]
    for copy in copies:
        copy.start()
    for copy in copies:
        copy.wait()


def per_device(hidden_in, lengths, w_qkv, w_attn_out, w_in, w_down, ln_gain, ln_bias):
    operands = (hidden_in, lengths, w_qkv, w_attn_out, w_in, w_down, ln_gain, ln_bias)
    made = layer(*(pltpu.with_memory_space_constraint(a, pltpu.HBM) for a in operands))
    return pl.pallas_call(
        hand_over,
        out_shape=tuple(jax.ShapeDtypeStruct(part.shape, part.dtype) for part in made),
        in_specs=[pl.BlockSpec(memory_space=pl.ANY)] * 3,
        out_specs=(pl.BlockSpec(memory_space=pltpu.HBM),) * 3,
        scratch_shapes=[pltpu.SemaphoreType.DMA((3,))],
        compiler_params=pltpu.CompilerParams(vmem_limit_bytes=1 << 20),
    )(*made)


def solution(mesh):
    rows = P(("seq", "head"), None)
    in_specs = (P(None, "seq", None), P(), rows, rows, rows, rows, P(), P())
    out_specs = (P(None, "seq", "head"),) * 3
    return jax.shard_map(per_device, mesh=mesh, in_specs=in_specs, out_specs=out_specs, check_vma=False)
```

```python
import math

import jax
import jax.numpy as jnp
from jax import lax
from jax.experimental import pallas as pl
from jax.experimental.pallas import tpu as pltpu
from jax.sharding import PartitionSpec as P

MESH = pl.DeviceIdType.MESH
BF = jnp.bfloat16
F32 = jnp.float32
EPSILON = 1e-05
SCORE_FACTOR = 64 ** (-0.5) * math.log2(math.e)
DEAD = -1e30
IN_X, IN_Z = 512, 640
DOWN_X, DOWN_Z = 384, 384


class Place:
    def __init__(self):
        self.s = lax.axis_index("seq")
        self.h = lax.axis_index("head")
        self.z = self.s // 8
        self.xl = lax.rem(self.s // 4, 2)
        self.y = lax.rem(self.s, 4)
        self.xh = self.h // 2
        self.c = lax.rem(self.h, 2)
        self.x = self.xh * 2 + self.xl

    def peer(self, dim, d):
        x, y, z = self.x, self.y, self.z
        if dim == "x":
            x = lax.rem(x + d, 4)
        elif dim == "y":
            y = lax.rem(y + d, 4)
        else:
            z = lax.rem(z + d, 4)
        return (z * 8 + lax.rem(x, 2) * 4 + y, (x // 2) * 2 + self.c)

    def sibling(self):
        return (self.s, self.xh * 2 + 1 - self.c)


def duty(s, h):
    z, xl, y = s // 8, lax.rem(s // 4, 2), lax.rem(s, 4)
    r = lax.rem(y + z + 2 * lax.rem(h, 2), 4)
    return z * 3 + r, xl, r < 3


def remote(src, dst, send, recv, device):
    return pltpu.make_async_remote_copy(
        src_ref=src, dst_ref=dst, send_sem=send, recv_sem=recv, device_id=device, device_id_type=MESH
    )


class Ring:
    def __init__(self, me, view, dim, send, recv):
        self.me, self.view, self.dim, self.send, self.recv = me, view, dim, send, recv
        self.copies = {}

    def half(self, way, step):
        return (step + way) % 2 if step < 2 else way

    def go(self, way, step):
        behind = 3 if way == 0 else 1
        part = self.view(0 if step < 2 else behind, self.half(way, step))
        copy = remote(
            part, part, self.send(way, step), self.recv(way, step), self.me.peer(self.dim, 1 if way == 0 else 3)
        )
        copy.start()
        self.copies[way, step] = copy

    def came(self, way, step):
        behind = 3 if way == 0 else 1
        return self.view(behind if step < 2 else 2, self.half(way, step))


def greet(barrier, device):
    pl.semaphore_signal(barrier, inc=1, device_id=device, device_id_type=MESH)


def normalize(rows, gain, shift):
    average = jnp.mean(rows, axis=1, keepdims=True)
    spread = jnp.mean(rows * rows, axis=1, keepdims=True) - average * average
    return (rows - average) * lax.rsqrt(spread + EPSILON) * gain + shift


def layer_kernel(
    x_hbm, len_ref, qkv_hbm, out_hbm, in_hbm, down_hbm, gain_ref, bias_ref, hidden_hbm, kc_hbm, vc_hbm,
    x_ref, qkv_f32, out_f32, in_f32, down_f32, other, qkv_half, in_half, out_half,
    slab, w_qkv, w_in, w_out, w_down, outbox, inbox, q_aug, k_aug, v_aug, attended, joined, hidden, result,
    caches, load_sem, swap_send, swap_recv, one_send, one_recv, two_send, two_recv, three_send, three_recv,
    box_own, box_send, box_recv, cache_sem, first_send, first_recv, ring_send, ring_recv,
    share_send, share_recv, mix_send, mix_recv, mix_own, back_send, back_recv, back_own,
):
    me = Place()
    prompt, pair, busy = duty(me.s, me.h)
    sibling = me.sibling()
    loads = [
        pltpu.make_async_copy(source, target, load_sem.at[n])
        for n, (source, target) in enumerate(
            (
                (qkv_hbm, qkv_f32), (out_hbm, out_f32), (in_hbm, in_f32), (down_hbm, down_f32), (x_hbm, x_ref),
            )
        )
    ]
    for copy in loads[:4]:
        copy.start()
    barrier = pltpu.get_barrier_semaphore()

    def greet_seq(i, carry):
        greet(barrier, (lax.rem(me.s + i, 32), me.h))
        return carry

    greet(barrier, sibling)
    for xl in range(2):
        greet(barrier, (me.z * 8 + xl * 4 + me.y, (1 - me.xh) * 2 + me.c))
    lax.fori_loop(1, 32, greet_seq, 0)

    loads[0].wait()
    for k in range(2):
        for t in range(3):
            at = pl.multiple_of(t * 1024 + (2 * k + 1 - me.c) * 256, 256)
            other[:, k * 768 + t * 256 : k * 768 + (t + 1) * 256] = qkv_f32[:, pl.ds(at, 256)]
    loads[1].wait()
    loads[2].wait()
    there = 1 - me.c
    swaps = [
        remote(other, qkv_half, swap_send.at[0], swap_recv.at[0], sibling),
        remote(
            out_f32.at[:, pl.ds(pl.multiple_of(there * 512, 512), 512)],
            out_half, swap_send.at[1], swap_recv.at[1], sibling,
        ),
        remote(
            in_f32.at[:, pl.ds(pl.multiple_of(there * 2048, 2048), 2048)],
            in_half, swap_send.at[2], swap_recv.at[2], sibling,
        ),
    ]
    loads[3].wait()
    loads[4].start()
    w_down[me.z, me.xl, me.y, me.xh, me.c] = down_f32[...].astype(BF)
    pl.semaphore_wait(barrier, 34)
    for copy in swaps:
        copy.start()
    first = me.c == 0

    def stack(mine, sent):
        rows = jnp.concatenate([jnp.where(first, mine, sent), jnp.where(first, sent, mine)], axis=0)
        return rows.astype(BF)

    pending = []
    one_c = pl.ds(me.c, 1)

    def region(piece, zs, xls, ys, xhs):
        rows16, rows32 = pl.ds(0, 16), pl.ds(0, 32)
        if piece == 0:
            return w_out.at[one_c, zs, xls, ys, xhs, rows16, pl.ds(0, 512)]
        start, stop = cuts[piece]
        if piece < 4:
            return w_in.at[one_c, zs, xls, ys, xhs, rows16, pl.ds(start, stop - start)]
        return w_down.at[zs, xls, ys, xhs, one_c, rows32, pl.ds(start, stop - start)]

    cuts = {
        1: (0, IN_X), 2: (IN_X, IN_X + IN_Z), 3: (IN_X + IN_Z, 2048),
        4: (0, DOWN_X), 5: (DOWN_X, DOWN_X + DOWN_Z), 6: (DOWN_X + DOWN_Z, 1024),
    }
    order = {0: "yzx", 1: "yzx", 2: "xyz", 3: "zxy", 4: "yzx", 5: "xyz", 6: "zxy"}
    early, late = (0, 1, 2, 3), (4, 5, 6)
    pieces = early + late

    def area(piece, done, at=None, half=None):
        x, y, z = me.x, me.y, me.z
        if at is not None:
            dim, d = at
            x = lax.rem(x + d, 4) if dim == "x" else x
            y = lax.rem(y + d, 4) if dim == "y" else y
            z = lax.rem(z + d, 4) if dim == "z" else z
        zs = pl.ds(0, 4) if "z" in done else pl.ds(z, 1)
        ys = pl.ds(0, 4) if "y" in done else pl.ds(y, 1)
        xls = pl.ds(0, 2) if "x" in done else pl.ds(lax.rem(x, 2), 1)
        xhs = pl.ds(0, 2) if "x" in done else pl.ds(x // 2, 1)
        if half is not None:
            if "z" in done:
                zs = pl.ds(half * 2, 2)
            elif "y" in done:
                ys = pl.ds(half * 2, 2)
            else:
                xls = pl.ds(half, 1)
        return region(piece, zs, xls, ys, xhs)

    def send_first(group):
        started = []
        for piece in group:
            part = area(piece, "")
            for d in (1, 3, 2):
                copy = remote(
                    part, part, first_send.at[piece, d - 1], first_recv.at[piece, d - 1], me.peer(order[piece][0], d)
                )
                copy.start()
                started.append(copy)
                pending.append(copy)
        return started

    late_one = send_first(late)
    swaps[0].wait_recv()
    for k in range(2):
        for t in range(3):
            at = pl.multiple_of(t * 1024 + (2 * k + me.c) * 256, 256)
            cols = slice(k * 768 + t * 256, k * 768 + (t + 1) * 256)
            slab[k, :, t * 256 : (t + 1) * 256] = stack(qkv_f32[:, pl.ds(at, 256)], qkv_half[:, cols])
    w_qkv[me.z, me.xl, me.y, me.xh] = slab[me.xh]
    one = []
    for d in (1, 3, 2):
        target = me.peer("x", d)
        copy = remote(
            slab.at[target[1] // 2], w_qkv.at[me.z, me.xl, me.y, me.xh], one_send.at[d - 1], one_recv.at[d - 1], target
        )
        copy.start()
        one.append(copy)
    pending += one

    for n, (source, half, width, target) in enumerate(
        ((out_f32, out_half, 512, w_out), (in_f32, in_half, 2048, w_in))
    ):
        swaps[n + 1].wait_recv()
        mine = source[:, pl.ds(pl.multiple_of(me.c * width, width), width)]
        target[me.c, me.z, me.xl, me.y, me.xh] = stack(mine, half[...])

    shares = {}

    def share(piece, slot, part):
        copy = remote(part, part, share_send.at[piece, slot], share_recv.at[piece, slot], sibling)
        copy.start()
        shares[piece, slot] = copy
        pending.append(copy)

    rings = {}
    for piece in pieces:
        for phase in (1, 2):
            dims = order[piece]
            rings[piece, phase] = Ring(
                me,
                lambda d, half, piece=piece, dims=dims, phase=phase: area(piece, dims[:phase], (dims[phase], d), half),
                dims[phase],
                lambda way, step, piece=piece, phase=phase: ring_send.at[piece, phase - 1, way, step],
                lambda way, step, piece=piece, phase=phase: ring_recv.at[piece, phase - 1, way, step],
            )

    def start(which, step):
        for ring in which:
            for way in range(2):
                ring.go(way, step)

    def take(which, step):
        for ring in which:
            for way in range(2):
                ring.copies[way, step].wait_recv()
                if step == 0:
                    ring.go(way, 2)

    def ring_start(group, step):
        start([rings[piece, 2] for piece in group], step)

    def ring_take(group, step):
        for piece in group:
            ring = rings[piece, 2]
            take([ring], step)
            for way in range(2):
                share(piece, 1 + way * 3 + step, ring.came(way, step))

    bulk_one = send_first(early)
    middle = [rings[piece, 1] for piece in late]
    for copy in late_one:
        copy.wait_recv()
    start(middle, 0)
    start(middle, 1)
    for copy in one:
        copy.wait_recv()
    left, right = pl.ds(0, 384), pl.ds(384, 384)
    all2, all4, all16 = pl.ds(0, 2), pl.ds(0, 4), pl.ds(0, 16)
    zs, ys = pl.ds(me.z, 1), pl.ds(me.y, 1)
    two = []
    for d in (1, 3, 2):
        for k, (dim, cols) in enumerate((("y", left), ("z", right))):
            part = w_qkv.at[zs, all2, ys, all2, all16, cols]
            copy = remote(part, part, two_send.at[k, d - 1], two_recv.at[k, d - 1], me.peer(dim, d))
            copy.start()
            two.append(copy)
    pending += two
    for copy in bulk_one:
        copy.wait_recv()
    middle = [rings[piece, 1] for piece in early]
    start(middle, 0)
    start(middle, 1)
    middle = [rings[piece, 1] for piece in pieces]
    for copy in two:
        copy.wait_recv()

    def view_left(d, half):
        return w_qkv.at[pl.ds(lax.rem(me.z + d, 4), 1), all2, pl.ds(half * 2, 2), all2, all16, left]

    def view_right(d, half):
        return w_qkv.at[pl.ds(half * 2, 2), all2, pl.ds(lax.rem(me.y + d, 4), 1), all2, all16, right]

    three = [
        Ring(
            me, view, dim,
            lambda way, step, k=k: three_send.at[k, way, step],
            lambda way, step, k=k: three_recv.at[k, way, step],
        )
        for k, (view, dim) in enumerate(((view_left, "z"), (view_right, "y")))
    ]
    start(three, 0)
    start(three, 1)
    take(three, 0)
    take(middle, 0)
    loads[4].wait()
    take(three, 1)
    take(three, 2)

    for t in range(3):
        w = w_qkv[:, :, :, :, :, t * 256 : (t + 1) * 256].reshape(1024, 256)
        for g in range(2):
            rows = x_ref[g * 6 : (g + 1) * 6].reshape(384, 1024)
            got = jnp.dot(rows, w, preferred_element_type=F32)
            for q in range(6):
                p = g * 6 + q
                piece = got[q * 64 : (q + 1) * 64]
                if t > 0:
                    at = me.s * 64 + lax.broadcasted_iota(jnp.int32, (64, 256), 0)
                    piece = jnp.where(at < len_ref[p], piece, 0.0)
                piece = piece.astype(BF)
                if t > 0:
                    caches[t - 1, p] = piece
                outbox[p * 2, t] = piece[:, :128]
                outbox[p * 2 + 1, t] = piece[:, 128:]

    def post(i, carry):
        to = lax.rem(me.s + i, 32)
        their_prompt, their_pair, their_busy = duty(to, me.h)

        @pl.when(their_busy)
        def _():
            remote(
                outbox.at[their_prompt * 2 + their_pair], inbox.at[:, me.s], box_send, box_recv, (to, me.h)
            ).start()

        return carry

    lax.fori_loop(1, 32, post, 0)
    keeps = [
        pltpu.make_async_copy(caches.at[0], kc_hbm, cache_sem.at[0]),
        pltpu.make_async_copy(caches.at[1], vc_hbm, cache_sem.at[1]),
    ]
    for copy in keeps:
        copy.start()

    take(middle, 1)
    take(middle, 2)
    ring_start(early, 0)
    ring_start(early, 1)
    for piece in pieces:
        share(piece, 0, area(piece, order[piece][:2]))
    ring_take(early, 0)
    ring_start(late, 0)
    ring_take(early, 1)
    ring_start(late, 1)

    @pl.when(busy)
    def _():
        keep = pltpu.make_async_copy(outbox.at[prompt * 2 + pair], inbox.at[:, me.s], box_own)
        keep.start()
        keep.wait()
        arrived = inbox.at[:, pl.ds(0, 31)]
        pltpu.make_async_copy(arrived, arrived, box_recv).wait()
        lane = lax.broadcasted_iota(jnp.int32, (2048, 128), 1)
        place = lax.broadcasted_iota(jnp.int32, (2048, 128), 0)
        bias = jnp.where(place < len_ref[prompt], 0.0, DEAD)
        q = inbox[0].reshape(2048, 128).astype(F32)
        k = inbox[1].reshape(2048, 128).astype(F32)
        v = inbox[2].reshape(2048, 128).astype(F32)
        for n in range(2):
            own = (lane // 64) == n
            mark = lane == (1 - n) * 64
            q_aug[n] = jnp.where(own, q, jnp.where(mark, 1.0, 0.0)).astype(BF)
            k_aug[n] = jnp.where(mark, bias, k).astype(BF)
            v_aug[n] = jnp.where(own, v, 1.0).astype(BF)

    low = lax.broadcasted_iota(jnp.int32, (256, 128), 1) < 64
    columns = pl.ds(pl.multiple_of((me.h * 2 + pair) * 128, 128), 128)
    slot = lax.rem(prompt, 3)
    lands_here = me.h == me.z

    def attend(start, stop):
        @pl.when(busy)
        def _():
            def block(i, carry):
                rows = pl.ds(pl.multiple_of(i * 256, 256), 256)
                mixed = []
                for n in range(2):
                    scores = lax.dot_general(
                        q_aug[n, rows, :], k_aug[n], (((1,), (1,)), ((), ())), preferred_element_type=F32
                    )
                    top = jnp.max(scores, axis=1, keepdims=True)
                    terms = jnp.exp2((scores - top) * SCORE_FACTOR).astype(BF)
                    got = jnp.dot(terms, v_aug[n], preferred_element_type=F32)
                    mixed.append(got / pltpu.roll(got, 64, 1))
                both = jnp.where(low, mixed[0], mixed[1]).astype(BF)
                attended[pl.ds(i * 4, 4)] = both.reshape(4, 64, 128)
                for k in range(4):
                    to = i * 4 + k
                    stays = jnp.logical_and(lands_here, to == me.s)

                    @pl.when(stays)
                    def _():
                        pltpu.make_async_copy(attended.at[to], joined.at[slot, :, columns], mix_own).start()

                    @pl.when(jnp.logical_not(stays))
                    def _():
                        remote(
                            attended.at[to], joined.at[slot, :, columns], mix_send, mix_recv, (to, me.z)
                        ).start()

                return carry

            lax.fori_loop(start, stop, block, 0)

    attend(0, 2)
    ring_take(early, 2)
    attend(2, 7)
    ring_take(late, 0)
    attend(7, 8)
    ring_take(late, 1)
    mine_too = jnp.logical_and(busy, lands_here)

    @pl.when(mine_too)
    def _():
        pltpu.make_async_copy(attended.at[me.s], joined.at[slot, :, columns], mix_own).wait()
        part = attended.at[pl.ds(0, 23)]
        pltpu.make_async_copy(part, part, mix_recv).wait()

    @pl.when(jnp.logical_not(mine_too))
    def _():
        part = attended.at[pl.ds(0, 24)]
        pltpu.make_async_copy(part, part, mix_recv).wait()

    for key, copy in shares.items():
        if key[0] in early:
            copy.wait_recv()

    x_rows = x_ref[pl.ds(me.h * 3, 3)].reshape(192, 1024).astype(F32)
    mixed = joined[...].reshape(192, 1024)
    sums = jnp.concatenate(
        [jnp.dot(mixed, w_out[n].reshape(1024, 512), preferred_element_type=F32) for n in range(2)], axis=1
    )
    normed = normalize(sums + x_rows, gain_ref[0:1], bias_ref[0:1]).astype(BF)
    for n in range(2):
        for k in range(4):
            w = w_in[n, :, :, :, :, :, k * 512 : (k + 1) * 512].reshape(1024, 512)
            units = jnp.dot(normed, w, preferred_element_type=F32)
            units = 0.5 * units * (1.0 + lax.erf(units * (2.0**-0.5)))
            hidden[n * 4 + k] = units.astype(BF)
    ring_take(late, 2)
    for key, copy in shares.items():
        if key[0] in late:
            copy.wait_recv()
    total = normed.astype(F32)
    for k in range(8):
        w = w_down[k // 2, k % 2].reshape(512, 1024)
        total = total + jnp.dot(hidden[k], w, preferred_element_type=F32)
    final = normalize(total, gain_ref[1:2], bias_ref[1:2]).astype(BF)
    for n in range(4):
        result[n] = final[:, n * 256 : (n + 1) * 256].reshape(3, 64, 256)
    rows = pl.ds(me.h * 3, 3)
    own = pltpu.make_async_copy(result.at[me.h], hidden_hbm.at[rows], back_own)
    own.start()
    last = []
    for d in range(1, 4):
        to = lax.rem(me.h + d, 4)
        copy = remote(result.at[to], hidden_hbm.at[rows], back_send.at[d - 1], back_recv.at[d - 1], (me.s, to))
        copy.start()
        last.append(copy)

    @pl.when(busy)
    def _():
        gone = outbox.at[pl.ds(0, 23)]
        pltpu.make_async_copy(gone, gone, box_send).wait()

    @pl.when(jnp.logical_not(busy))
    def _():
        gone = outbox.at[pl.ds(0, 24)]
        pltpu.make_async_copy(gone, gone, box_send).wait()

    @pl.when(mine_too)
    def _():
        part = attended.at[pl.ds(0, 31)]
        pltpu.make_async_copy(part, part, mix_send).wait()

    @pl.when(jnp.logical_and(busy, jnp.logical_not(lands_here)))
    def _():
        pltpu.make_async_copy(attended, attended, mix_send).wait()

    for ring in [*rings.values(), *three]:
        pending += ring.copies.values()
    for copy in swaps + pending:
        copy.wait_send()
    for copy in keeps:
        copy.wait()
    own.wait()
    for copy in last:
        copy.wait()


def layer(x, lengths, w_qkv, w_attn_out, w_in, w_down, ln_gain, ln_bias):
    vmem, free = pl.BlockSpec(memory_space=pltpu.VMEM), pl.BlockSpec(memory_space=pl.ANY)
    hbm = pl.BlockSpec(memory_space=pltpu.HBM)
    dma = pltpu.SemaphoreType.DMA
    return pl.pallas_call(
        layer_kernel,
        out_shape=(jax.ShapeDtypeStruct((12, 64, 256), BF),) * 3,
        in_specs=[hbm, pl.BlockSpec(memory_space=pltpu.SMEM), hbm, hbm, hbm, hbm, vmem, vmem],
        out_specs=(free,) * 3,
        scratch_shapes=[
            pltpu.VMEM((12, 64, 1024), BF),
            pltpu.VMEM((8, 3072), F32),
            pltpu.VMEM((8, 1024), F32),
            pltpu.VMEM((8, 4096), F32),
            pltpu.VMEM((32, 1024), F32),
            pltpu.VMEM((8, 1536), F32),
            pltpu.VMEM((8, 1536), F32),
            pltpu.VMEM((8, 2048), F32),
            pltpu.VMEM((8, 512), F32),
            pltpu.VMEM((2, 16, 768), BF),
            pltpu.VMEM((4, 2, 4, 2, 16, 768), BF),
            pltpu.VMEM((2, 4, 2, 4, 2, 16, 2048), BF),
            pltpu.VMEM((2, 4, 2, 4, 2, 16, 512), BF),
            pltpu.VMEM((4, 2, 4, 2, 2, 32, 1024), BF),
            pltpu.VMEM((24, 3, 64, 128), BF),
            pltpu.VMEM((3, 32, 64, 128), BF),
            pltpu.VMEM((2, 2048, 128), BF),
            pltpu.VMEM((2, 2048, 128), BF),
            pltpu.VMEM((2, 2048, 128), BF),
            pltpu.VMEM((32, 64, 128), BF),
            pltpu.VMEM((3, 64, 1024), BF),
            pltpu.VMEM((8, 192, 512), BF),
            pltpu.VMEM((4, 3, 64, 256), BF),
            pltpu.VMEM((2, 12, 64, 256), BF),
            dma((5,)),
            dma((3,)),
            dma((3,)),
            dma((3,)),
            dma((3,)),
            dma((2, 3)),
            dma((2, 3)),
            dma((2, 2, 3)),
            dma((2, 2, 3)),
            dma,
            dma,
            dma,
            dma((2,)),
            dma((7, 3)),
            dma((7, 3)),
            dma((7, 2, 2, 3)),
            dma((7, 2, 2, 3)),
            dma((7, 7)),
            dma((7, 7)),
            dma,
            dma,
            dma,
            dma((3,)),
            dma((3,)),
            dma,
        ],
        compiler_params=pltpu.CompilerParams(collective_id=0, has_side_effects=True, vmem_limit_bytes=46 << 20),
    )(x, lengths, w_qkv, w_attn_out, w_in, w_down, ln_gain, ln_bias)


def hand_over(*refs):
    copies = [pltpu.make_async_copy(refs[n], refs[3 + n], refs[6].at[n]) for n in range(3)]
    for copy in copies:
        copy.start()
    for copy in copies:
        copy.wait()


def per_device(hidden_in, lengths, w_qkv, w_attn_out, w_in, w_down, ln_gain, ln_bias):
    operands = (hidden_in, lengths, w_qkv, w_attn_out, w_in, w_down, ln_gain, ln_bias)
    made = layer(*(pltpu.with_memory_space_constraint(a, pltpu.HBM) for a in operands))
    return pl.pallas_call(
        hand_over,
        out_shape=tuple(jax.ShapeDtypeStruct(part.shape, part.dtype) for part in made),
        in_specs=[pl.BlockSpec(memory_space=pl.ANY)] * 3,
        out_specs=(pl.BlockSpec(memory_space=pltpu.HBM),) * 3,
        scratch_shapes=[pltpu.SemaphoreType.DMA((3,))],
        compiler_params=pltpu.CompilerParams(vmem_limit_bytes=1 << 20),
    )(*made)


def solution(mesh):
    rows = P(("seq", "head"), None)
    in_specs = (P(None, "seq", None), P(), rows, rows, rows, rows, P(), P())
    out_specs = (P(None, "seq", "head"),) * 3
    return jax.shard_map(per_device, mesh=mesh, in_specs=in_specs, out_specs=out_specs, check_vma=False)
```

```python
import math

import jax
import jax.numpy as jnp
from jax import lax
from jax.experimental import pallas as pl
from jax.experimental.pallas import tpu as pltpu
from jax.sharding import PartitionSpec as P

MESH = pl.DeviceIdType.MESH
BF = jnp.bfloat16
F32 = jnp.float32
EPSILON = 1e-05
SCORE_FACTOR = 64 ** (-0.5) * math.log2(math.e)
DEAD = -1e30
IN_X, IN_Z = 512, 640
DOWN_X, DOWN_Z = 384, 384


class Place:
    def __init__(self):
        self.s = lax.axis_index("seq")
        self.h = lax.axis_index("head")
        self.z = self.s // 8
        self.xl = lax.rem(self.s // 4, 2)
        self.y = lax.rem(self.s, 4)
        self.xh = self.h // 2
        self.c = lax.rem(self.h, 2)
        self.x = self.xh * 2 + self.xl

    def peer(self, dim, d):
        x, y, z = self.x, self.y, self.z
        if dim == "x":
            x = lax.rem(x + d, 4)
        elif dim == "y":
            y = lax.rem(y + d, 4)
        else:
            z = lax.rem(z + d, 4)
        return (z * 8 + lax.rem(x, 2) * 4 + y, (x // 2) * 2 + self.c)

    def sibling(self):
        return (self.s, self.xh * 2 + 1 - self.c)


def duty(s, h):
    z, xl, y = s // 8, lax.rem(s // 4, 2), lax.rem(s, 4)
    r = lax.rem(y + z + 2 * lax.rem(h, 2), 4)
    return z * 3 + r, xl, r < 3


def remote(src, dst, send, recv, device):
    return pltpu.make_async_remote_copy(
        src_ref=src, dst_ref=dst, send_sem=send, recv_sem=recv, device_id=device, device_id_type=MESH
    )


class Ring:
    def __init__(self, me, view, dim, send, recv):
        self.me, self.view, self.dim, self.send, self.recv = me, view, dim, send, recv
        self.copies = {}

    def half(self, way, step):
        return (step + way) % 2 if step < 2 else way

    def go(self, way, step):
        behind = 3 if way == 0 else 1
        part = self.view(0 if step < 2 else behind, self.half(way, step))
        copy = remote(
            part, part, self.send(way, step), self.recv(way, step), self.me.peer(self.dim, 1 if way == 0 else 3)
        )
        copy.start()
        self.copies[way, step] = copy

    def came(self, way, step):
        behind = 3 if way == 0 else 1
        return self.view(behind if step < 2 else 2, self.half(way, step))


def greet(barrier, device):
    pl.semaphore_signal(barrier, inc=1, device_id=device, device_id_type=MESH)


def normalize(rows, gain, shift):
    average = jnp.mean(rows, axis=1, keepdims=True)
    spread = jnp.mean(rows * rows, axis=1, keepdims=True) - average * average
    return (rows - average) * lax.rsqrt(spread + EPSILON) * gain + shift


def layer_kernel(
    x_hbm, len_ref, qkv_hbm, out_hbm, in_hbm, down_hbm, gain_ref, bias_ref, hidden_hbm, kc_hbm, vc_hbm,
    x_ref, qkv_f32, out_f32, in_f32, down_f32, other, qkv_half, in_half, out_half,
    slab, w_qkv, w_in, w_out, w_down, outbox, inbox, q_aug, k_aug, v_aug, attended, joined, hidden, result,
    caches, load_sem, swap_send, swap_recv, one_send, one_recv, two_send, two_recv, three_send, three_recv,
    box_own, box_send, box_recv, cache_sem, first_send, first_recv, ring_send, ring_recv,
    share_send, share_recv, mix_send, mix_recv, mix_own, back_send, back_recv, back_own,
):
    me = Place()
    prompt, pair, busy = duty(me.s, me.h)
    sibling = me.sibling()
    loads = [
        pltpu.make_async_copy(source, target, load_sem.at[n])
        for n, (source, target) in enumerate(
            (
                (qkv_hbm, qkv_f32), (out_hbm, out_f32), (in_hbm, in_f32), (down_hbm, down_f32), (x_hbm, x_ref),
            )
        )
    ]
    for copy in loads[:4]:
        copy.start()
    barrier = pltpu.get_barrier_semaphore()

    def greet_seq(i, carry):
        greet(barrier, (lax.rem(me.s + i, 32), me.h))
        return carry

    greet(barrier, sibling)
    for xl in range(2):
        greet(barrier, (me.z * 8 + xl * 4 + me.y, (1 - me.xh) * 2 + me.c))
    lax.fori_loop(1, 32, greet_seq, 0)

    loads[0].wait()
    for k in range(2):
        for t in range(3):
            at = pl.multiple_of(t * 1024 + (2 * k + 1 - me.c) * 256, 256)
            other[:, k * 768 + t * 256 : k * 768 + (t + 1) * 256] = qkv_f32[:, pl.ds(at, 256)]
    loads[1].wait()
    loads[2].wait()
    there = 1 - me.c
    swaps = [
        remote(other, qkv_half, swap_send.at[0], swap_recv.at[0], sibling),
        remote(
            out_f32.at[:, pl.ds(pl.multiple_of(there * 512, 512), 512)],
            out_half, swap_send.at[1], swap_recv.at[1], sibling,
        ),
        remote(
            in_f32.at[:, pl.ds(pl.multiple_of(there * 2048, 2048), 2048)],
            in_half, swap_send.at[2], swap_recv.at[2], sibling,
        ),
    ]
    loads[3].wait()
    loads[4].start()
    w_down[me.z, me.xl, me.y, me.xh, me.c] = down_f32[...].astype(BF)
    pl.semaphore_wait(barrier, 34)
    for copy in swaps:
        copy.start()
    first = me.c == 0

    def stack(mine, sent):
        rows = jnp.concatenate([jnp.where(first, mine, sent), jnp.where(first, sent, mine)], axis=0)
        return rows.astype(BF)

    pending = []
    one_c = pl.ds(me.c, 1)

    def region(piece, zs, xls, ys, xhs):
        rows16, rows32 = pl.ds(0, 16), pl.ds(0, 32)
        if piece == 0:
            return w_out.at[one_c, zs, xls, ys, xhs, rows16, pl.ds(0, 512)]
        start, stop = cuts[piece]
        if piece < 4:
            return w_in.at[one_c, zs, xls, ys, xhs, rows16, pl.ds(start, stop - start)]
        return w_down.at[zs, xls, ys, xhs, one_c, rows32, pl.ds(start, stop - start)]

    cuts = {
        1: (0, IN_X), 2: (IN_X, IN_X + IN_Z), 3: (IN_X + IN_Z, 2048),
        4: (0, DOWN_X), 5: (DOWN_X, DOWN_X + DOWN_Z), 6: (DOWN_X + DOWN_Z, 1024),
    }
    order = {0: "yzx", 1: "yzx", 2: "xyz", 3: "zxy", 4: "yzx", 5: "xyz", 6: "zxy"}
    early, late = (0, 1, 2, 3), (4, 5, 6)
    pieces = late + early

    def area(piece, done, at=None, half=None):
        x, y, z = me.x, me.y, me.z
        if at is not None:
            dim, d = at
            x = lax.rem(x + d, 4) if dim == "x" else x
            y = lax.rem(y + d, 4) if dim == "y" else y
            z = lax.rem(z + d, 4) if dim == "z" else z
        zs = pl.ds(0, 4) if "z" in done else pl.ds(z, 1)
        ys = pl.ds(0, 4) if "y" in done else pl.ds(y, 1)
        xls = pl.ds(0, 2) if "x" in done else pl.ds(lax.rem(x, 2), 1)
        xhs = pl.ds(0, 2) if "x" in done else pl.ds(x // 2, 1)
        if half is not None:
            if "z" in done:
                zs = pl.ds(half * 2, 2)
            elif "y" in done:
                ys = pl.ds(half * 2, 2)
            else:
                xls = pl.ds(half, 1)
        return region(piece, zs, xls, ys, xhs)

    def send_first(group):
        started = []
        for piece in group:
            part = area(piece, "")
            for d in (1, 3, 2):
                copy = remote(
                    part, part, first_send.at[piece, d - 1], first_recv.at[piece, d - 1], me.peer(order[piece][0], d)
                )
                copy.start()
                started.append(copy)
                pending.append(copy)
        return started

    late_one = send_first(late)
    swaps[0].wait_recv()
    for k in range(2):
        for t in range(3):
            at = pl.multiple_of(t * 1024 + (2 * k + me.c) * 256, 256)
            cols = slice(k * 768 + t * 256, k * 768 + (t + 1) * 256)
            slab[k, :, t * 256 : (t + 1) * 256] = stack(qkv_f32[:, pl.ds(at, 256)], qkv_half[:, cols])
    w_qkv[me.z, me.xl, me.y, me.xh] = slab[me.xh]
    one = []
    for d in (1, 3, 2):
        target = me.peer("x", d)
        copy = remote(
            slab.at[target[1] // 2], w_qkv.at[me.z, me.xl, me.y, me.xh], one_send.at[d - 1], one_recv.at[d - 1], target
        )
        copy.start()
        one.append(copy)
    pending += one

    for n, (source, half, width, target) in enumerate(
        ((out_f32, out_half, 512, w_out), (in_f32, in_half, 2048, w_in))
    ):
        swaps[n + 1].wait_recv()
        mine = source[:, pl.ds(pl.multiple_of(me.c * width, width), width)]
        target[me.c, me.z, me.xl, me.y, me.xh] = stack(mine, half[...])

    shares = {}

    def share(piece, slot, part):
        copy = remote(part, part, share_send.at[piece, slot], share_recv.at[piece, slot], sibling)
        copy.start()
        shares[piece, slot] = copy
        pending.append(copy)

    rings = {}
    for piece in pieces:
        for phase in (1, 2):
            dims = order[piece]
            rings[piece, phase] = Ring(
                me,
                lambda d, half, piece=piece, dims=dims, phase=phase: area(piece, dims[:phase], (dims[phase], d), half),
                dims[phase],
                lambda way, step, piece=piece, phase=phase: ring_send.at[piece, phase - 1, way, step],
                lambda way, step, piece=piece, phase=phase: ring_recv.at[piece, phase - 1, way, step],
            )

    def start(which, step):
        for ring in which:
            for way in range(2):
                ring.go(way, step)

    def take(which, step):
        for ring in which:
            for way in range(2):
                ring.copies[way, step].wait_recv()
                if step == 0:
                    ring.go(way, 2)

    def ring_start(group, step):
        start([rings[piece, 2] for piece in group], step)

    def ring_take(group, step):
        for piece in group:
            ring = rings[piece, 2]
            take([ring], step)
            for way in range(2):
                share(piece, 1 + way * 3 + step, ring.came(way, step))

    bulk_one = send_first(early)
    middle = [rings[piece, 1] for piece in late]
    for copy in late_one:
        copy.wait_recv()
    start(middle, 0)
    start(middle, 1)
    for copy in one:
        copy.wait_recv()
    left, right = pl.ds(0, 384), pl.ds(384, 384)
    all2, all4, all16 = pl.ds(0, 2), pl.ds(0, 4), pl.ds(0, 16)
    zs, ys = pl.ds(me.z, 1), pl.ds(me.y, 1)
    two = []
    for d in (1, 3, 2):
        for k, (dim, cols) in enumerate((("y", left), ("z", right))):
            part = w_qkv.at[zs, all2, ys, all2, all16, cols]
            copy = remote(part, part, two_send.at[k, d - 1], two_recv.at[k, d - 1], me.peer(dim, d))
            copy.start()
            two.append(copy)
    pending += two
    for copy in bulk_one:
        copy.wait_recv()
    middle = [rings[piece, 1] for piece in early]
    start(middle, 0)
    start(middle, 1)
    middle = [rings[piece, 1] for piece in pieces]
    for copy in two:
        copy.wait_recv()

    def view_left(d, half):
        return w_qkv.at[pl.ds(lax.rem(me.z + d, 4), 1), all2, pl.ds(half * 2, 2), all2, all16, left]

    def view_right(d, half):
        return w_qkv.at[pl.ds(half * 2, 2), all2, pl.ds(lax.rem(me.y + d, 4), 1), all2, all16, right]

    three = [
        Ring(
            me, view, dim,
            lambda way, step, k=k: three_send.at[k, way, step],
            lambda way, step, k=k: three_recv.at[k, way, step],
        )
        for k, (view, dim) in enumerate(((view_left, "z"), (view_right, "y")))
    ]
    start(three, 0)
    start(three, 1)
    take(three, 0)
    take(middle, 0)
    loads[4].wait()
    take(three, 1)
    take(three, 2)

    for t in range(3):
        w = w_qkv[:, :, :, :, :, t * 256 : (t + 1) * 256].reshape(1024, 256)
        for g in range(2):
            rows = x_ref[g * 6 : (g + 1) * 6].reshape(384, 1024)
            got = jnp.dot(rows, w, preferred_element_type=F32)
            for q in range(6):
                p = g * 6 + q
                piece = got[q * 64 : (q + 1) * 64]
                if t > 0:
                    at = me.s * 64 + lax.broadcasted_iota(jnp.int32, (64, 256), 0)
                    piece = jnp.where(at < len_ref[p], piece, 0.0)
                piece = piece.astype(BF)
                if t > 0:
                    caches[t - 1, p] = piece
                outbox[p * 2, t] = piece[:, :128]
                outbox[p * 2 + 1, t] = piece[:, 128:]

    def post(i, carry):
        to = lax.rem(me.s + i, 32)
        their_prompt, their_pair, their_busy = duty(to, me.h)

        @pl.when(their_busy)
        def _():
            remote(
                outbox.at[their_prompt * 2 + their_pair], inbox.at[:, me.s], box_send, box_recv, (to, me.h)
            ).start()

        return carry

    lax.fori_loop(1, 32, post, 0)
    keeps = [
        pltpu.make_async_copy(caches.at[0], kc_hbm, cache_sem.at[0]),
        pltpu.make_async_copy(caches.at[1], vc_hbm, cache_sem.at[1]),
    ]
    for copy in keeps:
        copy.start()

    take(middle, 1)
    take(middle, 2)
    ring_start(early, 0)
    ring_start(early, 1)
    for piece in pieces:
        share(piece, 0, area(piece, order[piece][:2]))
    ring_take(early, 0)
    ring_start(late, 0)
    ring_take(early, 1)
    ring_start(late, 1)

    @pl.when(busy)
    def _():
        keep = pltpu.make_async_copy(outbox.at[prompt * 2 + pair], inbox.at[:, me.s], box_own)
        keep.start()
        keep.wait()
        arrived = inbox.at[:, pl.ds(0, 31)]
        pltpu.make_async_copy(arrived, arrived, box_recv).wait()
        lane = lax.broadcasted_iota(jnp.int32, (2048, 128), 1)
        place = lax.broadcasted_iota(jnp.int32, (2048, 128), 0)
        bias = jnp.where(place < len_ref[prompt], 0.0, DEAD)
        q = inbox[0].reshape(2048, 128).astype(F32)
        k = inbox[1].reshape(2048, 128).astype(F32)
        v = inbox[2].reshape(2048, 128).astype(F32)
        for n in range(2):
            own = (lane // 64) == n
            mark = lane == (1 - n) * 64
            q_aug[n] = jnp.where(own, q, jnp.where(mark, 1.0, 0.0)).astype(BF)
            k_aug[n] = jnp.where(mark, bias, k).astype(BF)
            v_aug[n] = jnp.where(own, v, 1.0).astype(BF)

    low = lax.broadcasted_iota(jnp.int32, (256, 128), 1) < 64
    columns = pl.ds(pl.multiple_of((me.h * 2 + pair) * 128, 128), 128)
    slot = lax.rem(prompt, 3)
    lands_here = me.h == me.z

    def attend(start, stop):
        @pl.when(busy)
        def _():
            def block(i, carry):
                rows = pl.ds(pl.multiple_of(i * 256, 256), 256)
                mixed = []
                for n in range(2):
                    scores = lax.dot_general(
                        q_aug[n, rows, :], k_aug[n], (((1,), (1,)), ((), ())), preferred_element_type=F32
                    )
                    top = jnp.max(scores, axis=1, keepdims=True)
                    terms = jnp.exp2((scores - top) * SCORE_FACTOR).astype(BF)
                    got = jnp.dot(terms, v_aug[n], preferred_element_type=F32)
                    mixed.append(got / pltpu.roll(got, 64, 1))
                both = jnp.where(low, mixed[0], mixed[1]).astype(BF)
                attended[pl.ds(i * 4, 4)] = both.reshape(4, 64, 128)
                for k in range(4):
                    to = i * 4 + k
                    stays = jnp.logical_and(lands_here, to == me.s)

                    @pl.when(stays)
                    def _():
                        pltpu.make_async_copy(attended.at[to], joined.at[slot, :, columns], mix_own).start()

                    @pl.when(jnp.logical_not(stays))
                    def _():
                        remote(
                            attended.at[to], joined.at[slot, :, columns], mix_send, mix_recv, (to, me.z)
                        ).start()

                return carry

            lax.fori_loop(start, stop, block, 0)

    attend(0, 2)
    ring_take(early, 2)
    attend(2, 7)
    ring_take(late, 0)
    attend(7, 8)
    ring_take(late, 1)
    mine_too = jnp.logical_and(busy, lands_here)

    @pl.when(mine_too)
    def _():
        pltpu.make_async_copy(attended.at[me.s], joined.at[slot, :, columns], mix_own).wait()
        part = attended.at[pl.ds(0, 23)]
        pltpu.make_async_copy(part, part, mix_recv).wait()

    @pl.when(jnp.logical_not(mine_too))
    def _():
        part = attended.at[pl.ds(0, 24)]
        pltpu.make_async_copy(part, part, mix_recv).wait()

    for key, copy in shares.items():
        if key[0] in early:
            copy.wait_recv()

    x_rows = x_ref[pl.ds(me.h * 3, 3)].reshape(192, 1024).astype(F32)
    mixed = joined[...].reshape(192, 1024)
    sums = jnp.concatenate(
        [jnp.dot(mixed, w_out[n].reshape(1024, 512), preferred_element_type=F32) for n in range(2)], axis=1
    )
    normed = normalize(sums + x_rows, gain_ref[0:1], bias_ref[0:1]).astype(BF)
    for n in range(2):
        for k in range(4):
            w = w_in[n, :, :, :, :, :, k * 512 : (k + 1) * 512].reshape(1024, 512)
            units = jnp.dot(normed, w, preferred_element_type=F32)
            units = 0.5 * units * (1.0 + lax.erf(units * (2.0**-0.5)))
            hidden[n * 4 + k] = units.astype(BF)
    ring_take(late, 2)
    for key, copy in shares.items():
        if key[0] in late:
            copy.wait_recv()
    total = normed.astype(F32)
    for k in range(8):
        w = w_down[k // 2, k % 2].reshape(512, 1024)
        total = total + jnp.dot(hidden[k], w, preferred_element_type=F32)
    final = normalize(total, gain_ref[1:2], bias_ref[1:2]).astype(BF)
    for n in range(4):
        result[n] = final[:, n * 256 : (n + 1) * 256].reshape(3, 64, 256)
    rows = pl.ds(me.h * 3, 3)
    own = pltpu.make_async_copy(result.at[me.h], hidden_hbm.at[rows], back_own)
    own.start()
    last = []
    for d in (2, 3, 1):
        to = lax.rem(me.h + d, 4)
        copy = remote(result.at[to], hidden_hbm.at[rows], back_send.at[d - 1], back_recv.at[d - 1], (me.s, to))
        copy.start()
        last.append(copy)

    @pl.when(busy)
    def _():
        gone = outbox.at[pl.ds(0, 23)]
        pltpu.make_async_copy(gone, gone, box_send).wait()

    @pl.when(jnp.logical_not(busy))
    def _():
        gone = outbox.at[pl.ds(0, 24)]
        pltpu.make_async_copy(gone, gone, box_send).wait()

    @pl.when(mine_too)
    def _():
        part = attended.at[pl.ds(0, 31)]
        pltpu.make_async_copy(part, part, mix_send).wait()

    @pl.when(jnp.logical_and(busy, jnp.logical_not(lands_here)))
    def _():
        pltpu.make_async_copy(attended, attended, mix_send).wait()

    for ring in [*rings.values(), *three]:
        pending += ring.copies.values()
    for copy in swaps + pending:
        copy.wait_send()
    for copy in keeps:
        copy.wait()
    own.wait()
    for copy in last:
        copy.wait()


def layer(x, lengths, w_qkv, w_attn_out, w_in, w_down, ln_gain, ln_bias):
    vmem, free = pl.BlockSpec(memory_space=pltpu.VMEM), pl.BlockSpec(memory_space=pl.ANY)
    hbm = pl.BlockSpec(memory_space=pltpu.HBM)
    dma = pltpu.SemaphoreType.DMA
    return pl.pallas_call(
        layer_kernel,
        out_shape=(jax.ShapeDtypeStruct((12, 64, 256), BF),) * 3,
        in_specs=[hbm, pl.BlockSpec(memory_space=pltpu.SMEM), hbm, hbm, hbm, hbm, vmem, vmem],
        out_specs=(free,) * 3,
        scratch_shapes=[
            pltpu.VMEM((12, 64, 1024), BF),
            pltpu.VMEM((8, 3072), F32),
            pltpu.VMEM((8, 1024), F32),
            pltpu.VMEM((8, 4096), F32),
            pltpu.VMEM((32, 1024), F32),
            pltpu.VMEM((8, 1536), F32),
            pltpu.VMEM((8, 1536), F32),
            pltpu.VMEM((8, 2048), F32),
            pltpu.VMEM((8, 512), F32),
            pltpu.VMEM((2, 16, 768), BF),
            pltpu.VMEM((4, 2, 4, 2, 16, 768), BF),
            pltpu.VMEM((2, 4, 2, 4, 2, 16, 2048), BF),
            pltpu.VMEM((2, 4, 2, 4, 2, 16, 512), BF),
            pltpu.VMEM((4, 2, 4, 2, 2, 32, 1024), BF),
            pltpu.VMEM((24, 3, 64, 128), BF),
            pltpu.VMEM((3, 32, 64, 128), BF),
            pltpu.VMEM((2, 2048, 128), BF),
            pltpu.VMEM((2, 2048, 128), BF),
            pltpu.VMEM((2, 2048, 128), BF),
            pltpu.VMEM((32, 64, 128), BF),
            pltpu.VMEM((3, 64, 1024), BF),
            pltpu.VMEM((8, 192, 512), BF),
            pltpu.VMEM((4, 3, 64, 256), BF),
            pltpu.VMEM((2, 12, 64, 256), BF),
            dma((5,)),
            dma((3,)),
            dma((3,)),
            dma((3,)),
            dma((3,)),
            dma((2, 3)),
            dma((2, 3)),
            dma((2, 2, 3)),
            dma((2, 2, 3)),
            dma,
            dma,
            dma,
            dma((2,)),
            dma((7, 3)),
            dma((7, 3)),
            dma((7, 2, 2, 3)),
            dma((7, 2, 2, 3)),
            dma((7, 7)),
            dma((7, 7)),
            dma,
            dma,
            dma,
            dma((3,)),
            dma((3,)),
            dma,
        ],
        compiler_params=pltpu.CompilerParams(collective_id=0, has_side_effects=True, vmem_limit_bytes=46 << 20),
    )(x, lengths, w_qkv, w_attn_out, w_in, w_down, ln_gain, ln_bias)


def hand_over(*refs):
    copies = [pltpu.make_async_copy(refs[n], refs[3 + n], refs[6].at[n]) for n in range(3)]
    for copy in copies:
        copy.start()
    for copy in copies:
        copy.wait()


def per_device(hidden_in, lengths, w_qkv, w_attn_out, w_in, w_down, ln_gain, ln_bias):
    operands = (hidden_in, lengths, w_qkv, w_attn_out, w_in, w_down, ln_gain, ln_bias)
    made = layer(*(pltpu.with_memory_space_constraint(a, pltpu.HBM) for a in operands))
    return pl.pallas_call(
        hand_over,
        out_shape=tuple(jax.ShapeDtypeStruct(part.shape, part.dtype) for part in made),
        in_specs=[pl.BlockSpec(memory_space=pl.ANY)] * 3,
        out_specs=(pl.BlockSpec(memory_space=pltpu.HBM),) * 3,
        scratch_shapes=[pltpu.SemaphoreType.DMA((3,))],
        compiler_params=pltpu.CompilerParams(vmem_limit_bytes=1 << 20),
    )(*made)


def solution(mesh):
    rows = P(("seq", "head"), None)
    in_specs = (P(None, "seq", None), P(), rows, rows, rows, rows, P(), P())
    out_specs = (P(None, "seq", "head"),) * 3
    return jax.shard_map(per_device, mesh=mesh, in_specs=in_specs, out_specs=out_specs, check_vma=False)
```
